32 devices in a mesh: dp: 8 (over z, y), mp: 4 (over x, core).
Axes of the slice: x: 2, y: 2, z: 4, core: 2. Of those that a mesh axis runs over, the one named last changes fastest.
Arguments:
- suffix: bfloat16 [3584, 768], P('dp'), may hold values from -6 to 6
- memory: bfloat16 [28672, 768], P('dp'), may hold values from -6 to 6
- cotangent: bfloat16 [3584, 768], P('dp'), may hold values from -6 to 6
- group_kind: int32 [112], P('dp'), may hold values 0 or 1
- prefix_len: int32 [112], P('dp'), may hold values from 1 to 32
- suffix_len: int32 [112], P('dp'), may hold values from 1 to 32
- gain_self: float32 [768], replicated, may hold values from 0.25 to 1.75
- shift_self: float32 [768], replicated, may hold values from -2 to 2
- gain_cross: float32 [768], replicated, may hold values from 0.25 to 1.75
- shift_cross: float32 [768], replicated, may hold values from -2 to 2
- gain_mlp: float32 [768], replicated, may hold values from 0.25 to 1.75
- shift_mlp: float32 [768], replicated, may hold values from -2 to 2
- self_query: bfloat16 [768, 768], P(None, 'mp'), may hold values from -0.21875 to 0.21875
- self_key: bfloat16 [768, 768], P(None, 'mp'), may hold values from -0.21875 to 0.21875
- self_value: bfloat16 [768, 768], P(None, 'mp'), may hold values from -0.21875 to 0.21875
- self_out: bfloat16 [768, 768], P('mp'), may hold values from -0.875 to 0.875
- cross_query: bfloat16 [768, 768], P(None, 'mp'), may hold values from -0.21875 to 0.21875
- cross_key: bfloat16 [768, 768], P(None, 'mp'), may hold values from -0.21875 to 0.21875
- cross_value: bfloat16 [768, 768], P(None, 'mp'), may hold values from -0.21875 to 0.21875
- cross_out: bfloat16 [768, 768], P('mp'), may hold values from -1.75 to 1.75
- mlp_up: bfloat16 [768, 3072], P(None, 'mp'), may hold values from -0.21875 to 0.21875
- mlp_down: bfloat16 [3072, 768], P('mp'), may hold values from -0.109375 to 0.109375
Outputs:
- layer_out: bfloat16 [3584, 768], P('dp')
- suffix_grad: bfloat16 [3584, 768], P('dp')
- memory_grad: bfloat16 [28672, 768], P('dp')
- grad_self_query: float32 [768, 768], P('dp', 'mp')
- grad_self_key: float32 [768, 768], P('dp', 'mp')
- grad_self_value: float32 [768, 768], P('dp', 'mp')
- grad_self_out: float32 [768, 768], P('mp', 'dp')
- grad_cross_query: float32 [768, 768], P('dp', 'mp')
- grad_cross_key: float32 [768, 768], P('dp', 'mp')
- grad_cross_value: float32 [768, 768], P('dp', 'mp')
- grad_cross_out: float32 [768, 768], P('mp', 'dp')
- grad_mlp_up: float32 [768, 3072], P('dp', 'mp')
- grad_mlp_down: float32 [3072, 768], P('mp', 'dp')
- grad_gain_self: float32 [768], P('dp')
- grad_shift_self: float32 [768], P('dp')
- grad_gain_cross: float32 [768], P('dp')
- grad_shift_cross: float32 [768], P('dp')
- grad_gain_mlp: float32 [768], P('dp')
- grad_shift_mlp: float32 [768], P('dp')
The draws below stay inside these ranges and needn't reach their ends.
Inputs may be any that keep to these rules, and one draw needn't show every extreme that they name: `group_kind`: 1 marks an image-text group, whose memory holds 196 patches and then its prefix; 0 a text-only group, whose memory holds its prefix only. memory slot j of a group is live when j < 196 * group_kind + prefix_len. suffix positions at or past suffix_len are padding and are never attended to.
All inputs are finite; a program needn't handle non-finite values.
Results may differ from the reference program's by a relative error of at most 0.019.
Values may be sent and summed in bfloat16 or wider, within the bound.
A program may use at most 128 MiB of HBM per device.

```python
import jax
import jax.numpy as jnp
from jax import lax

D = 768
HEAD_DIM = 64
FF = 3072
SUFFIX = 32
PATCHES = 196
PREFIX = 32
MEM = 256
GROUPS_DEV = 14
GROUPS = 112
TOKENS = 3584
MEM_ROWS = 28672
N_DP = 8


def with_ends(drawn, own_key, low, top_value):
    longest = drawn.shape.index(max(drawn.shape))
    spots = []
    for shift in (0, 1):
        where = [jax.random.randint(jax.random.fold_in(own_key, axis), (), 0, length) for axis, length in enumerate(drawn.shape)]
        where[longest] = (where[longest] + shift) % drawn.shape[longest]
        spots.append(tuple(where))
    return drawn.at[spots[0]].set(low).at[spots[1]].set(top_value)


def strengthened(values, own_key, source, target, parts, factor):
    def block_of(axis_at):
        return (jnp.arange(values.shape[axis_at]) // (values.shape[axis_at] // parts)).reshape((-1,) + (1,) * (values.ndim - 1 - axis_at))

    one_side = jax.random.permutation(own_key, parts)[block_of(target)]
    second = (block_of(target) + parts // 2) % parts
    return jnp.where((block_of(source) == one_side) | (block_of(source) == second), factor * values, values)


def levels(stream_key, shape, cuts, smallest, largest):
    loudness = 1.0
    for dim, blocks in cuts:
        draws = jax.random.uniform(jax.random.fold_in(jax.random.fold_in(stream_key, 6), dim), (blocks,), jnp.float32, smallest / len(cuts), largest / len(cuts))
        loudness = loudness * jnp.repeat(jnp.exp(draws), shape[dim] // blocks).reshape((-1,) + (1,) * (len(shape) - 1 - dim))
    return loudness


def normal_values(key, dims, scale, most, split=(), kind=jnp.bfloat16):
    values = scale * jax.random.normal(key, dims, jnp.float32)
    if split:
        values = values * levels(key, dims, split, -0.22, 0.18)
    return jnp.clip(values, -most, most).astype(kind)


def noise_with(key, dims, deviation, bound, cuts, heavy, dtype=jnp.bfloat16):
    entries = deviation * jax.random.normal(key, dims, jnp.float32)
    if cuts:
        entries = entries * levels(key, dims, cuts, -0.22, 0.18)
    return jnp.clip(strengthened(entries, jax.random.fold_in(key, 3), *heavy), -bound, bound).astype(dtype)


def setup_inputs(seed: int = 0) -> dict:
    key_of = jax.random.split(jax.random.key(seed), 23)
    return {
        "suffix": noise_with(key_of[0], (TOKENS, D), 1.0, 6.0, ((0, 8),), (0, 1, 8, 2.0)),
        "memory": noise_with(key_of[1], (MEM_ROWS, D), 1.0, 6.0, ((0, 8),), (0, 1, 8, 2.0)),
        "cotangent": noise_with(key_of[2], (TOKENS, D), 1.0, 6.0, ((0, 8),), (0, 1, 8, 2.0)),
        "group_kind": with_ends((jax.random.randint(key_of[3], (GROUPS,), 0, 2) < 1).astype(jnp.int32), jax.random.fold_in(key_of[3], 1), 0, 1),
        "prefix_len": with_ends(jax.random.randint(key_of[4], (GROUPS,), 1, PREFIX + 1), jax.random.fold_in(key_of[4], 1), 1, PREFIX).astype(jnp.int32),
        "suffix_len": with_ends(jax.random.randint(key_of[5], (GROUPS,), 1, SUFFIX + 1), jax.random.fold_in(key_of[5], 1), 1, SUFFIX).astype(jnp.int32),
        "gain_self": jnp.clip(1.0 + 0.15 * jax.random.normal(key_of[6], (D,), jnp.float32), 0.25, 1.75),
        "shift_self": normal_values(key_of[7], (D,), 0.3, 2.0, (), jnp.float32),
        "gain_cross": jnp.clip(1.0 + 0.15 * jax.random.normal(key_of[8], (D,), jnp.float32), 0.25, 1.75),
        "shift_cross": normal_values(key_of[9], (D,), 0.3, 2.0, (), jnp.float32),
        "gain_mlp": jnp.clip(1.0 + 0.15 * jax.random.normal(key_of[10], (D,), jnp.float32), 0.25, 1.75),
        "shift_mlp": normal_values(key_of[11], (D,), 0.3, 2.0, (), jnp.float32),
        "self_query": normal_values(key_of[12], (D, D), D ** -0.5, 0.21875, ((1, 4),)),
        "self_key": normal_values(key_of[13], (D, D), D ** -0.5, 0.21875, ((1, 4),)),
        "self_value": normal_values(key_of[14], (D, D), D ** -0.5, 0.21875, ((1, 4),)),
        "self_out": normal_values(key_of[15], (D, D), (D // 16) ** -0.5, 0.875, ((0, 4),)),
        "cross_query": normal_values(key_of[16], (D, D), D ** -0.5, 0.21875, ((1, 4),)),
        "cross_key": normal_values(key_of[17], (D, D), D ** -0.5, 0.21875, ((1, 4),)),
        "cross_value": normal_values(key_of[18], (D, D), D ** -0.5, 0.21875, ((1, 4),)),
        "cross_out": normal_values(key_of[19], (D, D), (D // 64) ** -0.5, 1.75, ((0, 4),)),
        "mlp_up": normal_values(key_of[20], (D, FF), D ** -0.5, 0.21875, ((1, 4),)),
        "mlp_down": normal_values(key_of[21], (FF, D), FF ** -0.5, 0.109375, ((0, 4),)),
    }


EPSILON = 1e-06
NEG_FILL = -1e+30
PRECISE = lax.Precision.HIGHEST

@jax.custom_vjp
def low(v):
    return lax.optimization_barrier(v.astype(jnp.bfloat16)).astype(jnp.float32)

@jax.custom_vjp
def low_back(v):
    return v

def low_keep(v):
    return (low(v), None)

def low_pass(kept, grad):
    return (grad,)

def back_keep(v):
    return (v, None)

def back_low(kept, grad):
    return (low(grad),)
low.defvjp(low_keep, low_pass)
low_back.defvjp(back_keep, back_low)

def product(left_side, right_side):
    return jnp.dot(left_side, right_side, precision=PRECISE)

def layer_norm(vector, gain_row, shift_row):
    centred = vector - lax.optimization_barrier(jnp.mean(vector, axis=-1, keepdims=True))
    spread = lax.optimization_barrier(jnp.mean(centred * centred, axis=-1, keepdims=True))
    return centred * lax.rsqrt(spread + EPSILON) * gain_row + shift_row

def build_masks(group_kinds, prefixes, lengths):
    places = jnp.arange(SUFFIX)
    memory_slots = jnp.arange(MEM)
    self_mask = (places[None, :, None] >= places[None, None, :]) & (places[None, None, :] < lengths[:, None, None])
    reach_len = group_kinds * PATCHES + prefixes
    cross_mask = memory_slots[None, None, :] < reach_len[:, None, None]
    return (self_mask, cross_mask)

def attend(queries, keys_in, values_in, allowed):
    groups = allowed.shape[0]
    head_count = queries.shape[1] // HEAD_DIM
    query_heads = queries.reshape(groups, -1, head_count, HEAD_DIM)
    key_heads = keys_in.reshape(groups, -1, head_count, HEAD_DIM)
    value_heads = values_in.reshape(groups, -1, head_count, HEAD_DIM)
    scores = jnp.einsum('gqhe,gkhe->ghqk', query_heads, key_heads, precision=PRECISE) * HEAD_DIM ** (-0.5)
    scores = low_back(scores)
    scores = jnp.where(allowed[:, None], scores, NEG_FILL)
    weights = low(jax.nn.softmax(scores, axis=-1))
    mixed_out = jnp.einsum('ghqk,gkhe->gqhe', weights, value_heads, precision=PRECISE)
    return low(low_back(mixed_out.reshape(queries.shape)))

def decoder_layer(inputs, memories, group_kinds, prefixes, lengths, params):
    gain_self, shift_self, gain_cross, shift_cross, gain_mlp, shift_mlp, self_query, self_key, self_value, self_out, cross_query, cross_key, cross_value, cross_out, mlp_up, mlp_down = params
    self_mask, cross_mask = build_masks(group_kinds, prefixes, lengths)
    normed_one = low(layer_norm(inputs, gain_self, shift_self))
    query_one = low(low_back(product(normed_one, self_query)))
    key_one = low(low_back(product(normed_one, self_key)))
    value_one = low(low_back(product(normed_one, self_value)))
    hidden_one = inputs + low_back(product(attend(query_one, key_one, value_one, self_mask), self_out))
    normed_two = low(layer_norm(hidden_one, gain_cross, shift_cross))
    query_two = low(low_back(product(normed_two, cross_query)))
    key_two = low(low_back(product(memories, cross_key)))
    value_two = low(low_back(product(memories, cross_value)))
    hidden_two = hidden_one + low_back(product(attend(query_two, key_two, value_two, cross_mask), cross_out))
    normed_three = low(layer_norm(hidden_two, gain_mlp, shift_mlp))
    pre_act = low_back(product(normed_three, mlp_up))
    activated = low(jax.nn.gelu(pre_act, approximate=False))
    return hidden_two + low_back(product(activated, mlp_down))

def reference(suffix, memory, cotangent, group_kind, prefix_len, suffix_len, gain_self, shift_self, gain_cross, shift_cross, gain_mlp, shift_mlp, self_query, self_key, self_value, self_out, cross_query, cross_key, cross_value, cross_out, mlp_up, mlp_down):
    params = tuple((weight_item.astype(jnp.float32) for weight_item in (gain_self, shift_self, gain_cross, shift_cross, gain_mlp, shift_mlp, self_query, self_key, self_value, self_out, cross_query, cross_key, cross_value, cross_out, mlp_up, mlp_down)))
    block_rows = GROUPS_DEV * SUFFIX
    inputs = suffix.astype(jnp.float32).reshape(N_DP, block_rows, D)
    memories = memory.astype(jnp.float32).reshape(N_DP, GROUPS_DEV * MEM, D)
    group_kinds = group_kind.reshape(N_DP, GROUPS_DEV)
    prefixes = prefix_len.reshape(N_DP, GROUPS_DEV)
    lengths = suffix_len.reshape(N_DP, GROUPS_DEV)

    def forward(inputs, memories, params):

        def one_block(pieces):
            return jax.checkpoint(decoder_layer)(pieces[0], pieces[1], pieces[2], pieces[3], pieces[4], params)
        return lax.map(one_block, (inputs, memories, group_kinds, prefixes, lengths))
    result, pullback = jax.vjp(forward, inputs, memories, params)
    incoming_grad = cotangent.astype(jnp.float32).reshape(N_DP, block_rows, D)
    grad_inputs, grad_memories, grad_params = pullback(incoming_grad)
    g_gain_self, g_shift_self, g_gain_cross, g_shift_cross, g_gain_mlp, g_shift_mlp, g_self_query, g_self_key, g_self_value, g_self_out, g_cross_query, g_cross_key, g_cross_value, g_cross_out, g_mlp_up, g_mlp_down = grad_params
    return (result.reshape(N_DP * block_rows, D).astype(jnp.bfloat16), grad_inputs.reshape(N_DP * block_rows, D).astype(jnp.bfloat16), grad_memories.reshape(N_DP * GROUPS_DEV * MEM, D).astype(jnp.bfloat16), g_self_query, g_self_key, g_self_value, g_self_out, g_cross_query, g_cross_key, g_cross_value, g_cross_out, g_mlp_up, g_mlp_down, g_gain_self, g_shift_self, g_gain_cross, g_shift_cross, g_gain_mlp, g_shift_mlp)
```

```python
import math

import jax
import jax.numpy as jnp
from jax import lax
from jax.experimental import pallas as pl
from jax.experimental.pallas import tpu as pltpu
from jax.sharding import PartitionSpec as P

BF = jnp.bfloat16
F32 = jnp.float32
MESH = pl.DeviceIdType.MESH
HEAD = 64
PATCHES = 196
EPSILON = 1e-06
NEG_FILL = -1e30
UNIT = 384
ROWS = 32
N_SEMS = 160


def nn(a, b):
    return lax.dot_general(a, b, (((1,), (0,)), ((), ())), preferred_element_type=F32)


def nt(a, b):
    return lax.dot_general(a, b, (((1,), (1,)), ((), ())), preferred_element_type=F32)


def tn(a, b):
    return lax.dot_general(a, b, (((0,), (0,)), ((), ())), preferred_element_type=F32)


def normalize(v):
    centred = v - jnp.mean(v, axis=-1, keepdims=True)
    inverse = lax.rsqrt(jnp.mean(centred * centred, axis=-1, keepdims=True) + EPSILON)
    return centred * inverse, inverse


def norm_back(unit, inverse, gain, incoming):
    w = incoming * gain
    return inverse * (
        w - jnp.mean(w, axis=-1, keepdims=True) - unit * jnp.mean(w * unit, axis=-1, keepdims=True)
    )


def softmax(s):
    p = jnp.exp(s - jnp.max(s, axis=-1, keepdims=True))
    return p * (1.0 / jnp.sum(p, axis=-1, keepdims=True))


def fold8(v):
    total = v[0:8]
    for k in range(8, v.shape[0], 8):
        total = total + v[k : k + 8]
    return total


class Dims:
    def __init__(self, n_dp, n_mp, suffix, memory, group_kind, self_query, mlp_up):
        assert n_mp == 4
        self.n_dp = n_dp
        self.T, self.D = suffix.shape
        self.M = memory.shape[0]
        self.G = group_kind.shape[0]
        self.C = self_query.shape[1]
        self.F = mlp_up.shape[1]
        self.H = n_mp * self.C
        self.S = self.T // self.G
        self.K = self.M // self.G
        self.GO, self.RO, self.MO = self.G // 2, self.T // 2, self.M // 2
        self.NB = self.H // 256
        self.BLK = pl.cdiv(self.T, 128)
        self.TP = self.BLK * 128
        self.bits = n_dp.bit_length() - 1
        assert 1 << self.bits == n_dp
        halvings = 0
        while halvings < self.bits and (self.D >> (halvings + 1)) % 16 == 0:
            halvings += 1
        self.halvings = halvings
        self.low = self.bits - halvings
        self.nch = 1 << halvings
        self.rp = self.D // self.nch


UNITS = ("d1", "d2", "u1", "u2", "s1", "s2", "c1", "c2")
IN_NAMES = (
    "suffix",
    "memory",
    "cotangent",
    "kind",
    "prefix",
    "slen",
    "gain_self",
    "shift_self",
    "gain_cross",
    "shift_cross",
    "gain_mlp",
    "shift_mlp",
    "self_query",
    "self_key",
    "self_value",
    "self_out",
    "cross_query",
    "cross_key",
    "cross_value",
    "cross_out",
    "mlp_up",
    "mlp_down",
)
OUT_NAMES = (
    "layer_out",
    "suffix_grad",
    "memory_grad",
    "g_sq",
    "g_sk",
    "g_sv",
    "g_so",
    "g_cq",
    "g_ck",
    "g_cv",
    "g_co",
    "g_up",
    "g_dn",
    "norms",
)


def scratch(d):
    s = {}
    T, D, C, F, H, RO, MO, K = d.T, d.D, d.C, d.F, d.H, d.RO, d.MO, d.K

    def vmem(name, shape, dtype=BF):
        s[name] = pltpu.VMEM(shape, dtype)

    vmem("xin", (T, D))
    vmem("cot", (T, D))
    vmem("mem", (MO, D))
    for n in ("raw_sq", "raw_sk", "raw_sv", "raw_cq", "raw_ck", "raw_cv"):
        vmem(n, (D, C))
    vmem("wqkv", (D, 3 * C))
    vmem("so", (C, D))
    for n in ("cq", "ck", "cv", "co"):
        vmem(n, (H, D))
    vmem("up", (D, F))
    vmem("dn", (F, D))
    vmem("a1", (T, D))
    for n in ("q1", "k1", "v1", "o1", "do1"):
        vmem(n, (d.TP, C))
    vmem("p1", (d.BLK, 3 * 128, 128))
    vmem("dqkv", (d.TP, 3 * C))
    for k in (1, 3, 4, 6):
        for n in ("s", "r", "xs", "xr"):
            vmem(f"{n}{k}", (RO, D))
    vmem("h1", (RO, D), F32)
    vmem("h2", (RO, D), F32)
    vmem("dh", (RO, D), F32)
    vmem("tmp", (RO, D), F32)
    vmem("a2", (RO, D))
    vmem("c2", (RO, D))
    for n in ("q2", "o2", "do2", "dq2"):
        vmem(n, (RO, H))
    for n in ("k2", "v2", "dk2", "dv2"):
        vmem(n, (MO, H))
    for n in ("p2", "ds2"):
        vmem(n, (d.GO * d.NB, 4 * d.S, K))
    vmem("a3", (T, D))
    vmem("c1", (T, D))
    vmem("act", (T, F))
    vmem("du", (T, F))
    vmem("dact", (T, F), F32)
    vmem("mg", (d.GO, K, D))
    vmem("lo", (RO, D))
    vmem("sg", (RO, D))
    for n in ("cs1", "cs2", "cr1", "cr2"):
        vmem(n, (d.nch, d.rp, UNIT))
    for u in UNITS:
        vmem("g_" + u + "_acc", (d.nch, d.rp, UNIT))
        for k in range(d.halvings):
            vmem(f"g_{u}_r{k}", (d.nch >> (k + 1), d.rp, UNIT))
        for k in range(d.low):
            vmem(f"g_{u}_x{k}", (d.rp, UNIT))
            vmem(f"g_{u}_y{k}", (d.rp, UNIT))
    vmem("nst", (2 + d.bits, 8, D), F32)
    vmem("nrc", (1 + d.bits, 8, D), F32)
    s["ss"] = pltpu.SemaphoreType.DMA((N_SEMS,))
    s["rs"] = pltpu.SemaphoreType.DMA((N_SEMS,))
    s["ls"] = pltpu.SemaphoreType.DMA((48,))
    return s


class Refs:
    pass


def kernel(d, names, *args):
    r = Refs()
    for name, ref in zip(names, args):
        setattr(r, name, ref)
    dp, mp = lax.axis_index("dp"), lax.axis_index("mp")
    core = lax.rem(mp, 2)
    sib = {"mp": mp + 1 - 2 * core}
    xmate = {"mp": lax.rem(mp + 2, 4)}
    own = pl.multiple_of(core * d.RO, 16)
    other = pl.multiple_of((1 - core) * d.RO, 16)
    own_rows, other_rows = pl.ds(own, d.RO), pl.ds(other, d.RO)
    factor = 1.0 / math.sqrt(HEAD)

    def bit_of(b):
        return lax.rem(dp // (1 << b), 2)

    def mate(b):
        return {"dp": dp + (1 << b) * (1 - 2 * bit_of(b))}

    state = {"r": 0, "l": 0}
    sends, locals_ = [], []

    def remote(src, dst, device, index=None):
        if index is None:
            index = state["r"]
            state["r"] += 1
        cp = pltpu.make_async_remote_copy(
            src_ref=src,
            dst_ref=dst,
            send_sem=r.ss.at[index],
            recv_sem=r.rs.at[index],
            device_id=device,
            device_id_type=MESH,
        )
        return cp

    def send(src, dst, device):
        cp = remote(src, dst, device)
        cp.start()
        sends.append(cp)
        return cp

    def load(src, dst):
        cp = pltpu.make_async_copy(src, dst, r.ls.at[state["l"]])
        state["l"] += 1
        cp.start()
        return cp

    ld = {}
    mp_rows = pl.ds(pl.multiple_of(mp * d.C, 16), d.C)
    ld["ck"] = load(r.cross_key, r.raw_ck)
    ld["cv"] = load(r.cross_value, r.raw_cv)
    ld["cq"] = load(r.cross_query, r.raw_cq)
    ld["co"] = load(r.cross_out, r.co.at[mp_rows])
    ld["xin"] = load(r.suffix, r.xin)
    ld["sq"] = load(r.self_query, r.raw_sq)
    ld["sk"] = load(r.self_key, r.raw_sk)
    ld["sv"] = load(r.self_value, r.raw_sv)
    ld["so"] = load(r.self_out, r.so)
    ld["cot"] = load(r.cotangent, r.cot)
    ld["dn"] = load(r.mlp_down, r.dn)
    ld["mem"] = load(r.memory.at[pl.ds(pl.multiple_of(core * d.MO, 16), d.MO)], r.mem)
    ld["up"] = load(r.mlp_up, r.up)

    barrier = pltpu.get_barrier_semaphore()
    mates = [sib, xmate] + [mate(b) for b in range(d.bits)]
    for device in mates:
        pl.semaphore_signal(barrier, inc=1, device_id=device, device_id_type=MESH)
    pl.semaphore_wait(barrier, len(mates))

    PC = d.C // 2
    piece = lax.rem(dp, 2)
    full = {"ck": r.ck, "cv": r.cv, "cq": r.cq, "co": r.co}
    raw = {"ck": r.raw_ck, "cv": r.raw_cv, "cq": r.raw_cq}
    xm = lax.rem(mp + 2, 4)
    gat = {}

    def part(ref, owner, which):
        return ref.at[pl.ds(pl.multiple_of(owner * d.C + which * PC, 16), PC)]

    def gather_start(w):
        ref = full[w]
        ld[w].wait()
        if w in raw:
            ref[mp_rows, :] = raw[w][...].T
        mine = part(ref, mp, piece)
        gat[w, "x"] = send(mine, mine, xmate)
        gat[w, "s"] = send(ref.at[mp_rows], ref.at[mp_rows], sib)

    def gather_x(w):
        gat[w, "x"].wait_recv()
        got = part(full[w], xm, piece)
        gat[w, "y"] = send(got, got, mate(0))
        gat[w, "sx"] = send(got, got, sib)

    def gather_y(w):
        gat[w, "y"].wait_recv()
        got = part(full[w], xm, 1 - piece)
        gat[w, "sy"] = send(got, got, sib)

    def gather_done(w):
        for k in ("s", "sx", "sy"):
            gat[w, k].wait_recv()

    for w in ("ck", "cv", "cq", "co"):
        gather_start(w)

    class Unit:
        def __init__(self, name, finish):
            self.name, self.finish, self.stage = name, finish, 0
            self.acc = getattr(r, f"g_{name}_acc")
            self.base = 0
            self.cp = None

        def store(self, value, lane):
            width = value.shape[1]
            for j in range(d.nch):
                p = sum(((j >> k) & 1) * (d.nch >> (k + 1)) for k in range(d.halvings))
                self.acc[p, :, lane : lane + width] = value[j * d.rp : (j + 1) * d.rp].astype(BF)

        def go(self):
            k = self.stage
            if k < d.halvings:
                half = d.nch >> (k + 1)
                b = d.low + k
                dst = getattr(r, f"g_{self.name}_r{k}")
                src = self.acc.at[pl.ds(self.base + (1 - bit_of(b)) * half, half)]
                self.cp = send(src, dst, mate(b))
            else:
                e = k - d.halvings
                x = getattr(r, f"g_{self.name}_x{e}")
                x[...] = self.value.astype(BF)
                self.cp = send(x, getattr(r, f"g_{self.name}_y{e}"), mate(e))

        def step(self):
            k = self.stage
            self.cp.wait_recv()
            if k < d.halvings:
                half = d.nch >> (k + 1)
                got = getattr(r, f"g_{self.name}_r{k}")
                base = self.base + bit_of(d.low + k) * half
                self.base = base
                if k < d.halvings - 1:
                    for j in range(half):
                        self.acc[base + j] = (
                            self.acc[base + j].astype(F32) + got[j].astype(F32)
                        ).astype(BF)
                else:
                    self.value = self.acc[base].astype(F32) + got[0].astype(F32)
            else:
                e = k - d.halvings
                x = getattr(r, f"g_{self.name}_x{e}")
                y = getattr(r, f"g_{self.name}_y{e}")
                self.value = x[...].astype(F32) + y[...].astype(F32)
            self.stage += 1
            if self.stage < d.bits:
                self.go()
            else:
                self.finish(self.value)

        def drain(self):
            while self.stage < d.bits:
                self.step()

    def fin_dn(lane):
        def f(v):
            r.g_dn[lane : lane + UNIT, :] = v.T

        return f

    def fin_up(lane):
        def f(v):
            r.g_up[:, lane : lane + UNIT] = v

        return f

    def fin_pair(left, right, turn):
        def f(v):
            left[...] = v[:, : d.C]
            right[...] = v[:, d.C :].T if turn else v[:, d.C :]

        return f

    units = {
        "d1": Unit("d1", fin_dn(0)),
        "d2": Unit("d2", fin_dn(UNIT)),
        "u1": Unit("u1", fin_up(0)),
        "u2": Unit("u2", fin_up(UNIT)),
        "s1": Unit("s1", fin_pair(r.g_sq, r.g_sk, False)),
        "s2": Unit("s2", fin_pair(r.g_sv, r.g_so, True)),
        "c1": Unit("c1", fin_pair(r.g_cq, r.g_co, True)),
        "c2": Unit("c2", fin_pair(r.g_ck, r.g_cv, False)),
    }

    def steps(*which):
        for u in which:
            if units[u].stage < d.bits:
                units[u].step()

    def reduce_rows(k, partial):
        s, got, xs, xr = (getattr(r, f"{n}{k}") for n in ("s", "r", "xs", "xr"))
        s[...] = partial(other_rows).astype(BF)
        cp = send(s, got, sib)
        value = partial(own_rows)
        cp.wait_recv()
        xs[...] = (value + got[...].astype(F32)).astype(BF)
        return send(xs, xr, xmate)

    def total(k, s):
        return getattr(r, f"xs{k}")[s, :].astype(F32) + getattr(r, f"xr{k}")[s, :].astype(F32)

    def row_loop(n, body, carry=0):
        def step(i, c):
            return body(pl.multiple_of(i * ROWS, ROWS), c)

        return lax.fori_loop(0, n // ROWS, step, carry)

    def vec(ref):
        return ref[...].reshape(1, d.D)

    def head_masks(width, count):
        col = lax.broadcasted_iota(jnp.int32, (1, width), 1)
        f = [((col >= HEAD * h) & (col < HEAD * h + HEAD)).astype(F32) for h in range(count)]
        return f, [m.astype(BF) for m in f]

    HC = d.C // HEAD
    hf1, hb1 = head_masks(d.C, HC)
    hf2, hb2 = head_masks(256, 4)

    def spread(v, masks):
        return jnp.concatenate([v * m for m in masks], axis=0)

    def gatherh(v, masks):
        n = v.shape[0] // len(masks)
        out = v[:n] * masks[0]
        for h in range(1, len(masks)):
            out = out + v[h * n : (h + 1) * n] * masks[h]
        return out

    for n in ("q1", "k1", "v1", "o1", "do1"):
        ref = getattr(r, n)
        ref[d.T :, :] = jnp.zeros((d.TP - d.T, d.C), BF)
    ld["xin"].wait()
    gain, shift = vec(r.gain_self), vec(r.shift_self)

    def norm_one(i, c):
        s = pl.ds(i, ROWS)
        z, _ = normalize(r.xin[s, :].astype(F32))
        r.a1[s, :] = (z * gain + shift).astype(BF)
        return c

    row_loop(d.T, norm_one)
    for k, n in enumerate(("sq", "sk", "sv")):
        ld[n].wait()
        r.wqkv[:, k * d.C : (k + 1) * d.C] = getattr(r, "raw_" + n)[...]
    qkv = nn(r.a1[...], r.wqkv[...])
    r.q1[: d.T, :] = (qkv[:, : d.C] * factor).astype(BF)
    r.k1[: d.T, :] = qkv[:, d.C : 2 * d.C].astype(BF)
    r.v1[: d.T, :] = qkv[:, 2 * d.C :].astype(BF)
    gather_x("ck")

    ri = lax.broadcasted_iota(jnp.int32, (128, 128), 0)
    ci = lax.broadcasted_iota(jnp.int32, (128, 128), 1)
    near = (jnp.right_shift(ri, 5) == jnp.right_shift(ci, 5)) & (ci <= ri)
    place = jnp.bitwise_and(ci, 31)
    per = 128 // d.S
    for t in range(d.BLK):
        lens = jnp.zeros((128, 128), jnp.int32)
        for k in range(per):
            g = t * per + k
            if g < d.G:
                lens = jnp.where(jnp.right_shift(ci, 5) == k, r.slen[g], lens)
        ok = near & (place < lens)
        b = pl.ds(t * 128, 128)
        scores = nt(spread(r.q1[b, :], hb1), r.k1[b, :])
        scores = jnp.concatenate(
            [jnp.where(ok, scores[h * 128 : (h + 1) * 128], NEG_FILL) for h in range(HC)], axis=0
        )
        p = softmax(scores).astype(BF)
        r.p1[t] = p
        r.o1[b, :] = gatherh(nn(p, r.v1[b, :]), hf1).astype(BF)
    gather_x("cv")
    ld["so"].wait()
    x1 = reduce_rows(1, lambda s: nn(r.o1[s, :], r.so[...]))
    gather_x("cq")
    gather_y("ck")

    ld["cot"].wait()
    ld["dn"].wait()
    r.dact[...] = nt(r.cot[...], r.dn[...])
    gather_y("cv")
    gather_x("co")
    ld["mem"].wait()
    gather_done("ck")
    big = d.MO // 4

    def project(w, dst):
        def body(i, c):
            s = pl.ds(pl.multiple_of(i * big, 16), big)
            dst[s, :] = nt(r.mem[s, :], w[...]).astype(BF)
            return c

        lax.fori_loop(0, 4, body, 0)

    project(r.ck, r.k2)
    gather_y("cq")
    gather_done("cv")
    project(r.cv, r.v2)
    gather_y("co")

    x1.wait_recv()
    gain, shift = vec(r.gain_cross), vec(r.shift_cross)

    def norm_two(i, c):
        s = pl.ds(i, ROWS)
        h1 = r.xin[pl.ds(pl.multiple_of(own + i, 16), ROWS), :].astype(F32) + total(1, s)
        r.h1[s, :] = h1
        z, _ = normalize(h1)
        r.a2[s, :] = (z * gain + shift).astype(BF)
        return c

    row_loop(d.RO, norm_two)
    gather_done("cq")
    r.q2[...] = (nt(r.a2[...], r.cq[...]) * factor).astype(BF)
    slot = lax.broadcasted_iota(jnp.int32, (4 * d.S, d.K), 1)

    def cross_forward(g, c):
        n = core * d.GO + g
        live = r.kind[n] * PATCHES + r.prefix[n]
        qs = pl.ds(pl.multiple_of(g * d.S, d.S), d.S)
        ks = pl.ds(pl.multiple_of(g * d.K, d.K), d.K)
        for b in range(d.NB):
            lanes = slice(256 * b, 256 * b + 256)
            scores = nt(spread(r.q2[qs, lanes], hb2), r.k2[ks, lanes])
            p = softmax(jnp.where(slot < live, scores, NEG_FILL)).astype(BF)
            r.p2[g * d.NB + b] = p
            r.o2[qs, lanes] = gatherh(nn(p, r.v2[ks, lanes]), hf2).astype(BF)
        return c

    lax.fori_loop(0, d.GO, cross_forward, 0)
    gather_done("co")
    r.tmp[...] = nn(r.o2[...], r.co[...])
    gain, shift = vec(r.gain_mlp), vec(r.shift_mlp)

    def norm_three(i, c):
        s = pl.ds(i, ROWS)
        h2 = r.h1[s, :] + r.tmp[s, :]
        r.h2[s, :] = h2
        z, _ = normalize(h2)
        r.a3[pl.ds(pl.multiple_of(own + i, 16), ROWS), :] = (z * gain + shift).astype(BF)
        return c

    row_loop(d.RO, norm_three)
    a3 = send(r.a3.at[own_rows], r.a3.at[own_rows], sib)

    ld["up"].wait()
    root = 1.0 / math.sqrt(2.0)
    bell = 1.0 / math.sqrt(2.0 * math.pi)

    def hidden(start):
        r.tmp[...] = nn(r.a3[pl.ds(start, d.RO), :], r.up[...])

        def body(i, c):
            u = r.tmp[pl.ds(i, ROWS), :]
            s = pl.ds(pl.multiple_of(start + i, 16), ROWS)
            half = 0.5 * (1.0 + lax.erf(u * root))
            r.act[s, :] = (u * half).astype(BF)
            slope = half + u * (bell * jnp.exp(-0.5 * u * u))
            r.du[s, :] = (r.dact[s, :] * slope).astype(BF)
            return c

        row_loop(d.RO, body)

    hidden(own)
    a3.wait_recv()
    hidden(other)
    x4 = reduce_rows(4, lambda s: nt(r.du[s, :], r.up[...]))
    for u, lane in (("d1", 0), ("d2", UNIT)):
        units[u].store(tn(r.cot[...], r.act[:, lane : lane + UNIT]), 0)
        units[u].go()
    for u, lane in (("u1", 0), ("u2", UNIT)):
        units[u].store(tn(r.a3[...], r.du[:, lane : lane + UNIT]), 0)
        units[u].go()
    x3 = reduce_rows(3, lambda s: nn(r.act[s, :], r.dn[...]))

    x4.wait_recv()
    gain = vec(r.gain_mlp)
    zero8 = jnp.zeros((8, d.D), F32)

    def back_three(i, c):
        gg, gs = c
        s = pl.ds(i, ROWS)
        e = total(4, s)
        z, inv = normalize(r.h2[s, :])
        dh = r.cot[pl.ds(pl.multiple_of(own + i, 16), ROWS), :].astype(F32) + norm_back(
            z, inv, gain, e
        )
        r.dh[s, :] = dh
        r.c2[s, :] = dh.astype(BF)
        return gg + fold8(e * z), gs + fold8(e)

    gain_mlp_grad, shift_mlp_grad = row_loop(d.RO, back_three, (zero8, zero8))
    r.do2[...] = nt(r.c2[...], r.co[...]).astype(BF)

    def cross_backward(g, c):
        qs = pl.ds(pl.multiple_of(g * d.S, d.S), d.S)
        ks = pl.ds(pl.multiple_of(g * d.K, d.K), d.K)
        for b in range(d.NB):
            lanes = slice(256 * b, 256 * b + 256)
            dp_ = nt(spread(r.do2[qs, lanes], hb2), r.v2[ks, lanes])
            p = r.p2[g * d.NB + b].astype(F32)
            t = p * dp_
            ds = (t - p * jnp.sum(t, axis=-1, keepdims=True)).astype(BF)
            r.ds2[g * d.NB + b] = ds
            r.dq2[qs, lanes] = (gatherh(nn(ds, r.k2[ks, lanes]), hf2) * factor).astype(BF)
        return c

    lax.fori_loop(0, d.GO, cross_backward, 0)
    r.tmp[...] = nn(r.dq2[...], r.cq[...])
    gain = vec(r.gain_cross)

    def back_two(i, c):
        gg, gs = c
        s = pl.ds(i, ROWS)
        e = r.tmp[s, :]
        z, inv = normalize(r.h1[s, :])
        dh = r.dh[s, :] + norm_back(z, inv, gain, e)
        r.dh[s, :] = dh
        r.c1[pl.ds(pl.multiple_of(own + i, 16), ROWS), :] = dh.astype(BF)
        return gg + fold8(e * z), gs + fold8(e)

    gain_cross_grad, shift_cross_grad = row_loop(d.RO, back_two, (zero8, zero8))
    c1 = send(r.c1.at[own_rows], r.c1.at[own_rows], sib)
    steps("d1", "d2")

    r.do1[own_rows, :] = nt(r.c1[own_rows, :], r.so[...]).astype(BF)
    c1.wait_recv()
    r.do1[other_rows, :] = nt(r.c1[other_rows, :], r.so[...]).astype(BF)
    for t in range(d.BLK):
        b = pl.ds(t * 128, 128)
        dom = spread(r.do1[b, :], hb1)
        dp_ = nt(dom, r.v1[b, :])
        pb = r.p1[t]
        p = pb.astype(F32)
        tt = p * dp_
        ds = (tt - p * jnp.sum(tt, axis=-1, keepdims=True)).astype(BF)
        dq = gatherh(nn(ds, r.k1[b, :]), hf1) * factor
        dk = tn(ds, spread(r.q1[b, :], hb1))
        dv = tn(pb, dom)
        r.dqkv[b, : d.C] = dq.astype(BF)
        r.dqkv[b, d.C : 2 * d.C] = dk.astype(BF)
        r.dqkv[b, 2 * d.C :] = dv.astype(BF)
    x6 = reduce_rows(6, lambda s: nt(r.dqkv[s, :], r.wqkv[...]))
    rows = slice(0, d.T)
    units["s1"].store(tn(r.a1[...], r.dqkv[rows, : 2 * d.C]), 0)
    units["s1"].go()
    units["s2"].store(tn(r.a1[...], r.dqkv[rows, 2 * d.C :]), 0)
    units["s2"].store(tn(r.c1[...], r.o1[rows, :]), d.C)
    units["s2"].go()
    steps("u1", "u2", "d1", "d2")

    def cross_keys(g, c):
        qs = pl.ds(pl.multiple_of(g * d.S, d.S), d.S)
        ks = pl.ds(pl.multiple_of(g * d.K, d.K), d.K)
        for b in range(d.NB):
            lanes = slice(256 * b, 256 * b + 256)
            j = g * d.NB + b
            r.dk2[ks, lanes] = tn(r.ds2[j], spread(r.q2[qs, lanes], hb2)).astype(BF)
            r.dv2[ks, lanes] = tn(r.p2[j], spread(r.do2[qs, lanes], hb2)).astype(BF)
        return c

    lax.fori_loop(0, d.GO, cross_keys, 0)
    pair = pl.ds(pl.multiple_of((mp // 2) * 2 * d.C, 128), 2 * d.C)

    def split_columns(unit, away, lane, value):
        left, right = value[:, : d.C], value[:, d.C :]
        first = core == 0
        unit.store(jnp.where(first, left, right), lane)
        away.store(jnp.where(first, right, left), lane)

    class Away:
        def __init__(self, ref):
            self.acc = ref

        store = Unit.store

    away1, away2 = Away(r.cs1), Away(r.cs2)
    split_columns(units["c1"], away1, 0, tn(r.a2[...], r.dq2[:, pair]))
    split_columns(units["c1"], away1, d.C, tn(r.c2[...], r.o2[:, pair]))
    cc1 = send(r.cs1, r.cr1, sib)
    split_columns(units["c2"], away2, 0, tn(r.mem[...], r.dk2[:, pair]))

    def merge(unit, cp, got):
        cp.wait_recv()
        for j in range(d.nch):
            unit.acc[j] = (unit.acc[j].astype(F32) + got[j].astype(F32)).astype(BF)
        unit.go()

    merge(units["c1"], cc1, r.cr1)
    split_columns(units["c2"], away2, d.C, tn(r.mem[...], r.dv2[:, pair]))
    cc2 = send(r.cs2, r.cr2, sib)
    steps("u1", "u2")

    x3.wait_recv()

    def finish_out(i, c):
        s = pl.ds(i, ROWS)
        r.lo[s, :] = (r.h2[s, :] + total(3, s)).astype(BF)
        return c

    row_loop(d.RO, finish_out)
    tail = [send(r.lo, r.layer_out.at[own_rows], sib)]
    locals_.append(load(r.lo, r.layer_out.at[own_rows]))
    merge(units["c2"], cc2, r.cr2)

    x6.wait_recv()
    gain = vec(r.gain_self)

    def back_one(i, c):
        gg, gs = c
        s = pl.ds(i, ROWS)
        e = total(6, s)
        z, inv = normalize(r.xin[pl.ds(pl.multiple_of(own + i, 16), ROWS), :].astype(F32))
        r.sg[s, :] = (r.dh[s, :] + norm_back(z, inv, gain, e)).astype(BF)
        return gg + fold8(e * z), gs + fold8(e)

    gain_self_grad, shift_self_grad = row_loop(d.RO, back_one, (zero8, zero8))
    tail.append(send(r.sg, r.suffix_grad.at[own_rows], sib))
    locals_.append(load(r.sg, r.suffix_grad.at[own_rows]))
    for k, v in enumerate(
        (
            gain_self_grad,
            shift_self_grad,
            gain_cross_grad,
            shift_cross_grad,
            gain_mlp_grad,
            shift_mlp_grad,
        )
    ):
        r.nst[0, k : k + 1, :] = jnp.sum(v, axis=0, keepdims=True)
    r.nst[0, 6:8, :] = jnp.zeros((2, d.D), F32)
    devices = [sib] + [mate(b) for b in range(d.bits)]
    ncp = send(r.nst.at[0], r.nrc.at[0], devices[0])

    def norm_step(k, cp):
        cp.wait_recv()
        r.nst[k + 1] = r.nst[k] + r.nrc[k]
        if k + 1 < len(devices):
            return send(r.nst.at[k + 1], r.nrc.at[k + 1], devices[k + 1])
        return None

    base_r, base_l = state["r"], state["l"]
    state["r"] += d.GO
    state["l"] += d.GO

    def memory_copies(g):
        rows = pl.ds(pl.multiple_of(core * d.MO + g * d.K, 16), d.K)
        there = remote(r.mg.at[g], r.memory_grad.at[rows], sib, base_r + g)
        here = pltpu.make_async_copy(r.mg.at[g], r.memory_grad.at[rows], r.ls.at[base_l + g])
        return there, here

    def memory_group(g, c):
        ks = pl.ds(pl.multiple_of(g * d.K, d.K), d.K)
        value = nn(r.dk2[ks, :], r.ck[...]) + nn(r.dv2[ks, :], r.cv[...])
        r.mg[g] = value.astype(BF)
        there, here = memory_copies(g)
        there.start()
        here.start()
        return c

    lax.fori_loop(0, d.GO, memory_group, 0)
    ncp = norm_step(0, ncp)
    steps("s1", "s2", "d1", "d2")
    k = 1
    while ncp is not None:
        ncp = norm_step(k, ncp)
        k += 1
        if k == 2:
            steps("c1", "c2")
        if k == 3:
            steps("s1", "s2")
    r.norms[...] = r.nst[len(devices)]
    order = ("d1", "d2", "u1", "u2", "s1", "s2", "c1", "c2")
    while any(units[u].stage < d.bits for u in order):
        for u in order:
            if units[u].stage < d.bits:
                units[u].step()
    for g in range(d.GO):
        there, here = memory_copies(g)
        there.wait_recv()
        there.wait_send()
        here.wait()
    for cp in locals_:
        cp.wait()
    for cp in tail:
        cp.wait_recv()
    for cp in sends:
        cp.wait_send()
    assert state["r"] <= N_SEMS


def solution(mesh):
    n_dp, n_mp = mesh.shape["dp"], mesh.shape["mp"]

    def on_device(*args):
        d = Dims(n_dp, n_mp, args[0], args[1], args[3], args[12], args[20])
        assert d.C * 2 == UNIT and d.F == 2 * UNIT
        scr = scratch(d)
        names = IN_NAMES + OUT_NAMES + tuple(scr)
        col, turned = (d.rp, d.C), (d.C, d.rp)
        shapes = [
            ((d.T, d.D), BF),
            ((d.T, d.D), BF),
            ((d.M, d.D), BF),
            (col, F32),
            (col, F32),
            (col, F32),
            (turned, F32),
            (col, F32),
            (col, F32),
            (col, F32),
            (turned, F32),
            ((d.rp, d.F), F32),
            ((d.F, d.rp), F32),
            ((8, d.D), F32),
        ]
        hbm, vmem = pl.BlockSpec(memory_space=pl.ANY), pl.BlockSpec(memory_space=pltpu.VMEM)
        smem = pl.BlockSpec(memory_space=pltpu.SMEM)

        def body(*refs):
            kernel(d, names, *refs)

        outs = pl.pallas_call(
            body,
            out_shape=[jax.ShapeDtypeStruct(*s) for s in shapes],
            in_specs=[hbm] * 3 + [smem] * 3 + [vmem] * 6 + [hbm] * 10,
            out_specs=[hbm] * 3 + [vmem] * 11,
            scratch_shapes=list(scr.values()),
            compiler_params=pltpu.CompilerParams(
                collective_id=0, has_side_effects=True, vmem_limit_bytes=67043328
            ),
            name="layer",
        )(*args)
        big, grads, norms = outs[:3], list(outs[3:13]), outs[13]
        dp = lax.axis_index("dp")
        rows = d.D // n_dp
        if d.low:
            start = lax.rem(dp, 1 << d.low) * rows
            for k, turn in enumerate((0, 0, 0, 1, 0, 0, 0, 1, 0, 1)):
                grads[k] = lax.dynamic_slice_in_dim(grads[k], start, rows, axis=turn)
        vectors = [lax.dynamic_slice_in_dim(norms[k], dp * rows, rows, axis=0) for k in range(6)]
        return (*big, *grads, *vectors)

    row, col, turn = P("dp", None), P("dp", "mp"), P("mp", "dp")
    wide, tall = P(None, "mp"), P("mp", None)
    in_specs = (row,) * 3 + (P("dp"),) * 3 + (P(),) * 6
    in_specs += (wide, wide, wide, tall, wide, wide, wide, tall, wide, tall)
    out_specs = (row,) * 3 + (col, col, col, turn, col, col, col, turn, col, turn)
    out_specs += (P("dp"),) * 6
    return jax.shard_map(
        on_device, mesh=mesh, in_specs=in_specs, out_specs=out_specs, check_vma=False
    )
```

```python
import math

import jax
import jax.numpy as jnp
from jax import lax
from jax.experimental import pallas as pl
from jax.experimental.pallas import tpu as pltpu
from jax.sharding import PartitionSpec as P

BF = jnp.bfloat16
F32 = jnp.float32
MESH = pl.DeviceIdType.MESH
HEAD = 64
PATCHES = 196
EPSILON = 1e-06
NEG_FILL = -1e30
UNIT = 384
ROWS = 32
N_SEMS = 160
VMEM_BYTES = 52 * 2**20


def nn(a, b):
    return lax.dot_general(a, b, (((1,), (0,)), ((), ())), preferred_element_type=F32)


def nt(a, b):
    return lax.dot_general(a, b, (((1,), (1,)), ((), ())), preferred_element_type=F32)


def tn(a, b):
    return lax.dot_general(a, b, (((0,), (0,)), ((), ())), preferred_element_type=F32)


def normalize(v):
    centred = v - jnp.mean(v, axis=-1, keepdims=True)
    inverse = lax.rsqrt(jnp.mean(centred * centred, axis=-1, keepdims=True) + EPSILON)
    return centred * inverse, inverse


def norm_back(unit, inverse, gain, incoming):
    w = incoming * gain
    return inverse * (
        w - jnp.mean(w, axis=-1, keepdims=True) - unit * jnp.mean(w * unit, axis=-1, keepdims=True)
    )


def softmax(s):
    p = jnp.exp(s - jnp.max(s, axis=-1, keepdims=True))
    return p * (1.0 / jnp.sum(p, axis=-1, keepdims=True))


def fold8(v):
    total = v[0:8]
    for k in range(8, v.shape[0], 8):
        total = total + v[k : k + 8]
    return total


class Dims:
    def __init__(self, n_dp, n_mp, suffix, memory, group_kind, self_query, mlp_up):
        assert n_mp == 4
        self.n_dp = n_dp
        self.T, self.D = suffix.shape
        self.M = memory.shape[0]
        self.G = group_kind.shape[0]
        self.C = self_query.shape[1]
        self.F = mlp_up.shape[1]
        self.H = n_mp * self.C
        self.S = self.T // self.G
        self.K = self.M // self.G
        self.GO, self.RO, self.MO = self.G // 2, self.T // 2, self.M // 2
        self.NB = self.H // 256
        self.BLK = pl.cdiv(self.T, 128)
        self.TP = self.BLK * 128
        self.bits = n_dp.bit_length() - 1
        assert 1 << self.bits == n_dp
        halvings = 0
        while halvings < self.bits and (self.D >> (halvings + 1)) % 16 == 0:
            halvings += 1
        self.halvings = halvings
        self.low = self.bits - halvings
        self.nch = 1 << halvings
        self.rp = self.D // self.nch


UNITS = ("d1", "d2", "u1", "u2", "s1", "s2", "c1", "c2")
IN_NAMES = (
    "suffix",
    "memory",
    "cotangent",
    "kind",
    "prefix",
    "slen",
    "gain_self",
    "shift_self",
    "gain_cross",
    "shift_cross",
    "gain_mlp",
    "shift_mlp",
    "self_query",
    "self_key",
    "self_value",
    "self_out",
    "cross_query",
    "cross_key",
    "cross_value",
    "cross_out",
    "mlp_up",
    "mlp_down",
)
OUT_NAMES = (
    "layer_out",
    "suffix_grad",
    "memory_grad",
    "g_sq",
    "g_sk",
    "g_sv",
    "g_so",
    "g_cq",
    "g_ck",
    "g_cv",
    "g_co",
    "g_up",
    "g_dn",
    "norms",
)


def scratch(d):
    s = {}
    T, D, C, F, H, RO, MO, K = d.T, d.D, d.C, d.F, d.H, d.RO, d.MO, d.K

    def vmem(name, shape, dtype=BF):
        s[name] = pltpu.VMEM(shape, dtype)

    vmem("xin", (T, D))
    vmem("cot", (T, D))
    vmem("mem", (MO, D))
    vmem("wqkv", (3 * C, D))
    vmem("so", (C, D))
    for n in ("cq", "ck", "cv", "co"):
        vmem(n, (H, D))
    vmem("up", (D, F))
    vmem("dn", (F, D))
    vmem("a1", (T, D))
    for n in ("q1", "k1", "v1", "o1", "do1"):
        vmem(n, (d.TP, C))
    vmem("p1", (d.BLK, 3 * 128, 128))
    vmem("dqkv", (d.TP, 3 * C))
    for k in (1, 3, 4, 6):
        for n in ("s", "r", "xs", "xr"):
            vmem(f"{n}{k}", (RO, D))
    vmem("h1", (RO, D), F32)
    vmem("h2", (RO, D), F32)
    vmem("dh", (RO, D), F32)
    vmem("tmp", (RO, D), F32)
    vmem("a2", (RO, D))
    vmem("c2", (RO, D))
    for n in ("q2", "o2", "do2", "dq2"):
        vmem(n, (RO, H))
    for n in ("k2", "v2"):
        vmem(n, (MO, H))
    for n in ("p2", "ds2"):
        vmem(n, (d.GO * d.NB, 4 * d.S, K))
    vmem("a3", (T, D))
    vmem("c1", (T, D))
    vmem("act", (T, F))
    vmem("du", (T, F))
    vmem("dact", (T, F), F32)
    for n in ("cs1", "cs2", "cr1", "cr2"):
        vmem(n, (d.nch, d.rp, UNIT))
    for u in UNITS:
        vmem("g_" + u + "_acc", (d.nch, d.rp, UNIT))
        for k in range(d.halvings):
            vmem(f"g_{u}_r{k}", (d.nch >> (k + 1), d.rp, UNIT))
        for k in range(d.low):
            vmem(f"g_{u}_x{k}", (d.rp, UNIT))
            vmem(f"g_{u}_y{k}", (d.rp, UNIT))
    vmem("nst", (2 + d.bits, 8, D), F32)
    vmem("nrc", (1 + d.bits, 8, D), F32)
    s["ss"] = pltpu.SemaphoreType.DMA((N_SEMS,))
    s["rs"] = pltpu.SemaphoreType.DMA((N_SEMS,))
    s["ls"] = pltpu.SemaphoreType.DMA((48,))
    return s


class Refs:
    pass


def kernel(d, names, *args):
    r = Refs()
    for name, ref in zip(names, args):
        setattr(r, name, ref)
    dp, mp = lax.axis_index("dp"), lax.axis_index("mp")
    core = lax.rem(mp, 2)
    sib = {"mp": mp + 1 - 2 * core}
    xmate = {"mp": lax.rem(mp + 2, 4)}
    own = pl.multiple_of(core * d.RO, 16)
    other = pl.multiple_of((1 - core) * d.RO, 16)
    own_rows, other_rows = pl.ds(own, d.RO), pl.ds(other, d.RO)
    factor = 1.0 / math.sqrt(HEAD)

    def bit_of(b):
        return lax.rem(dp // (1 << b), 2)

    def mate(b):
        return {"dp": dp + (1 << b) * (1 - 2 * bit_of(b))}

    state = {"r": 0, "l": 0}
    sends = []

    def remote(src, dst, device, index=None):
        if index is None:
            index = state["r"]
            state["r"] += 1
        cp = pltpu.make_async_remote_copy(
            src_ref=src,
            dst_ref=dst,
            send_sem=r.ss.at[index],
            recv_sem=r.rs.at[index],
            device_id=device,
            device_id_type=MESH,
        )
        return cp

    def send(src, dst, device):
        cp = remote(src, dst, device)
        cp.start()
        sends.append(cp)
        return cp

    def load(src, dst):
        cp = pltpu.make_async_copy(src, dst, r.ls.at[state["l"]])
        state["l"] += 1
        cp.start()
        return cp

    ld = {}
    mp_rows = pl.ds(pl.multiple_of(mp * d.C, 16), d.C)
    ld["ck"] = load(r.cross_key, r.ck.at[mp_rows])
    ld["cv"] = load(r.cross_value, r.cv.at[mp_rows])
    ld["cq"] = load(r.cross_query, r.cq.at[mp_rows])
    ld["co"] = load(r.cross_out, r.co.at[mp_rows])
    ld["xin"] = load(r.suffix, r.xin)
    ld["sq"] = load(r.self_query, r.wqkv.at[pl.ds(0, d.C)])
    ld["sk"] = load(r.self_key, r.wqkv.at[pl.ds(d.C, d.C)])
    ld["sv"] = load(r.self_value, r.wqkv.at[pl.ds(2 * d.C, d.C)])
    ld["so"] = load(r.self_out, r.so)
    ld["cot"] = load(r.cotangent, r.cot)
    ld["dn"] = load(r.mlp_down, r.dn)
    ld["mem"] = load(r.memory.at[pl.ds(pl.multiple_of(core * d.MO, 16), d.MO)], r.mem)
    ld["up"] = load(r.mlp_up, r.up)

    barrier = pltpu.get_barrier_semaphore()
    mates = [sib, xmate] + [mate(b) for b in range(d.bits)]
    for device in mates:
        pl.semaphore_signal(barrier, inc=1, device_id=device, device_id_type=MESH)
    pl.semaphore_wait(barrier, len(mates))

    PC = d.C // 2
    piece = lax.rem(dp, 2)
    full = {"ck": r.ck, "cv": r.cv, "cq": r.cq, "co": r.co}
    xm = lax.rem(mp + 2, 4)
    gat = {}

    def part(ref, owner, which):
        return ref.at[pl.ds(pl.multiple_of(owner * d.C + which * PC, 16), PC)]

    def gather_start(w):
        ref = full[w]
        ld[w].wait()
        mine = part(ref, mp, piece)
        gat[w, "x"] = send(mine, mine, xmate)
        gat[w, "s"] = send(ref.at[mp_rows], ref.at[mp_rows], sib)

    def gather_x(w):
        gat[w, "x"].wait_recv()
        got = part(full[w], xm, piece)
        gat[w, "y"] = send(got, got, mate(0))
        gat[w, "sx"] = send(got, got, sib)

    def gather_y(w):
        gat[w, "y"].wait_recv()
        got = part(full[w], xm, 1 - piece)
        gat[w, "sy"] = send(got, got, sib)

    def gather_done(w):
        for k in ("s", "sx", "sy"):
            gat[w, k].wait_recv()

    for w in ("ck", "cv", "cq", "co"):
        gather_start(w)

    class Unit:
        def __init__(self, name, finish):
            self.name, self.finish, self.stage = name, finish, 0
            self.acc = getattr(r, f"g_{name}_acc")
            self.base = 0
            self.cp = None

        def store(self, value, lane):
            width = value.shape[1]
            for j in range(d.nch):
                p = sum(((j >> k) & 1) * (d.nch >> (k + 1)) for k in range(d.halvings))
                self.acc[p, :, lane : lane + width] = value[j * d.rp : (j + 1) * d.rp].astype(BF)

        def go(self):
            k = self.stage
            if k < d.halvings:
                half = d.nch >> (k + 1)
                b = d.low + k
                dst = getattr(r, f"g_{self.name}_r{k}")
                src = self.acc.at[pl.ds(self.base + (1 - bit_of(b)) * half, half)]
                self.cp = send(src, dst, mate(b))
            else:
                e = k - d.halvings
                x = getattr(r, f"g_{self.name}_x{e}")
                x[...] = self.value.astype(BF)
                self.cp = send(x, getattr(r, f"g_{self.name}_y{e}"), mate(e))

        def step(self):
            k = self.stage
            self.cp.wait_recv()
            if k < d.halvings:
                half = d.nch >> (k + 1)
                got = getattr(r, f"g_{self.name}_r{k}")
                base = self.base + bit_of(d.low + k) * half
                self.base = base
                if k < d.halvings - 1:
                    for j in range(half):
                        self.acc[base + j] = (
                            self.acc[base + j].astype(F32) + got[j].astype(F32)
                        ).astype(BF)
                else:
                    self.value = self.acc[base].astype(F32) + got[0].astype(F32)
            else:
                e = k - d.halvings
                x = getattr(r, f"g_{self.name}_x{e}")
                y = getattr(r, f"g_{self.name}_y{e}")
                self.value = x[...].astype(F32) + y[...].astype(F32)
            self.stage += 1
            if self.stage < d.bits:
                self.go()
            else:
                self.finish(self.value)

        def drain(self):
            while self.stage < d.bits:
                self.step()

    def fin_dn(lane):
        def f(v):
            r.g_dn[:, lane : lane + UNIT] = v

        return f

    def fin_up(lane):
        def f(v):
            r.g_up[:, lane : lane + UNIT] = v

        return f

    def fin_pair(left, right, turn):
        def f(v):
            left[...] = v[:, : d.C]
            right[...] = v[:, d.C :].T if turn else v[:, d.C :]

        return f

    units = {
        "d1": Unit("d1", fin_dn(0)),
        "d2": Unit("d2", fin_dn(UNIT)),
        "u1": Unit("u1", fin_up(0)),
        "u2": Unit("u2", fin_up(UNIT)),
        "s1": Unit("s1", fin_pair(r.g_sq, r.g_sk, False)),
        "s2": Unit("s2", fin_pair(r.g_sv, r.g_so, True)),
        "c1": Unit("c1", fin_pair(r.g_cq, r.g_co, True)),
        "c2": Unit("c2", fin_pair(r.g_ck, r.g_cv, False)),
    }

    def steps(*which):
        for u in which:
            if units[u].stage < d.bits:
                units[u].step()

    def reduce_rows(k, partial):
        s, got, xs, xr = (getattr(r, f"{n}{k}") for n in ("s", "r", "xs", "xr"))
        s[...] = partial(other_rows).astype(BF)
        cp = send(s, got, sib)
        value = partial(own_rows)
        cp.wait_recv()
        xs[...] = (value + got[...].astype(F32)).astype(BF)
        return send(xs, xr, xmate)

    def total(k, s):
        return getattr(r, f"xs{k}")[s, :].astype(F32) + getattr(r, f"xr{k}")[s, :].astype(F32)

    def row_loop(n, body, carry=0):
        def step(i, c):
            return body(pl.multiple_of(i * ROWS, ROWS), c)

        return lax.fori_loop(0, n // ROWS, step, carry)

    def vec(ref):
        return ref[...].reshape(1, d.D)

    def head_masks(width, count):
        col = lax.broadcasted_iota(jnp.int32, (1, width), 1)
        f = [((col >= HEAD * h) & (col < HEAD * h + HEAD)).astype(F32) for h in range(count)]
        return f, [m.astype(BF) for m in f]

    HC = d.C // HEAD
    hf1, hb1 = head_masks(d.C, HC)
    hf2, hb2 = head_masks(256, 4)

    def spread(v, masks):
        return jnp.concatenate([v * m for m in masks], axis=0)

    def gatherh(v, masks):
        n = v.shape[0] // len(masks)
        out = v[:n] * masks[0]
        for h in range(1, len(masks)):
            out = out + v[h * n : (h + 1) * n] * masks[h]
        return out

    for n in ("q1", "k1", "v1", "o1", "do1"):
        ref = getattr(r, n)
        ref[d.T :, :] = jnp.zeros((d.TP - d.T, d.C), BF)
    ld["xin"].wait()
    gain, shift = vec(r.gain_self), vec(r.shift_self)

    def norm_one(i, c):
        s = pl.ds(i, ROWS)
        z, _ = normalize(r.xin[s, :].astype(F32))
        r.a1[s, :] = (z * gain + shift).astype(BF)
        return c

    row_loop(d.T, norm_one)
    for n in ("sq", "sk", "sv"):
        ld[n].wait()
    qkv = nt(r.a1[...], r.wqkv[...])
    r.q1[: d.T, :] = (qkv[:, : d.C] * factor).astype(BF)
    r.k1[: d.T, :] = qkv[:, d.C : 2 * d.C].astype(BF)
    r.v1[: d.T, :] = qkv[:, 2 * d.C :].astype(BF)
    gather_x("ck")

    ri = lax.broadcasted_iota(jnp.int32, (128, 128), 0)
    ci = lax.broadcasted_iota(jnp.int32, (128, 128), 1)
    near = (jnp.right_shift(ri, 5) == jnp.right_shift(ci, 5)) & (ci <= ri)
    place = jnp.bitwise_and(ci, 31)
    per = 128 // d.S
    for t in range(d.BLK):
        lens = jnp.zeros((128, 128), jnp.int32)
        for k in range(per):
            g = t * per + k
            if g < d.G:
                lens = jnp.where(jnp.right_shift(ci, 5) == k, r.slen[g], lens)
        ok = near & (place < lens)
        b = pl.ds(t * 128, 128)
        scores = nt(spread(r.q1[b, :], hb1), r.k1[b, :])
        scores = jnp.concatenate(
            [jnp.where(ok, scores[h * 128 : (h + 1) * 128], NEG_FILL) for h in range(HC)], axis=0
        )
        p = softmax(scores).astype(BF)
        r.p1[t] = p
        r.o1[b, :] = gatherh(nn(p, r.v1[b, :]), hf1).astype(BF)
    gather_x("cv")
    ld["so"].wait()
    x1 = reduce_rows(1, lambda s: nn(r.o1[s, :], r.so[...]))
    gather_x("cq")
    gather_y("ck")

    ld["cot"].wait()
    ld["dn"].wait()
    r.dact[...] = nt(r.cot[...], r.dn[...])
    gather_y("cv")
    gather_x("co")
    ld["mem"].wait()
    gather_done("ck")
    big = d.MO // 4

    def project(w, dst):
        def body(i, c):
            s = pl.ds(pl.multiple_of(i * big, 16), big)
            dst[s, :] = nt(r.mem[s, :], w[...]).astype(BF)
            return c

        lax.fori_loop(0, 4, body, 0)

    project(r.ck, r.k2)
    gather_y("cq")
    gather_done("cv")
    project(r.cv, r.v2)
    gather_y("co")

    x1.wait_recv()
    gain, shift = vec(r.gain_cross), vec(r.shift_cross)

    def norm_two(i, c):
        s = pl.ds(i, ROWS)
        h1 = r.xin[pl.ds(pl.multiple_of(own + i, 16), ROWS), :].astype(F32) + total(1, s)
        r.h1[s, :] = h1
        z, _ = normalize(h1)
        r.a2[s, :] = (z * gain + shift).astype(BF)
        return c

    row_loop(d.RO, norm_two)
    gather_done("cq")
    r.q2[...] = (nt(r.a2[...], r.cq[...]) * factor).astype(BF)
    slot = lax.broadcasted_iota(jnp.int32, (4 * d.S, d.K), 1)

    def cross_forward(g, c):
        n = core * d.GO + g
        live = r.kind[n] * PATCHES + r.prefix[n]
        qs = pl.ds(pl.multiple_of(g * d.S, d.S), d.S)
        ks = pl.ds(pl.multiple_of(g * d.K, d.K), d.K)
        for b in range(d.NB):
            lanes = slice(256 * b, 256 * b + 256)
            scores = nt(spread(r.q2[qs, lanes], hb2), r.k2[ks, lanes])
            p = softmax(jnp.where(slot < live, scores, NEG_FILL)).astype(BF)
            r.p2[g * d.NB + b] = p
            r.o2[qs, lanes] = gatherh(nn(p, r.v2[ks, lanes]), hf2).astype(BF)
        return c

    lax.fori_loop(0, d.GO, cross_forward, 0)
    gather_done("co")
    r.tmp[...] = nn(r.o2[...], r.co[...])
    gain, shift = vec(r.gain_mlp), vec(r.shift_mlp)

    def norm_three(i, c):
        s = pl.ds(i, ROWS)
        h2 = r.h1[s, :] + r.tmp[s, :]
        r.h2[s, :] = h2
        z, _ = normalize(h2)
        r.a3[pl.ds(pl.multiple_of(own + i, 16), ROWS), :] = (z * gain + shift).astype(BF)
        return c

    row_loop(d.RO, norm_three)
    a3 = send(r.a3.at[own_rows], r.a3.at[own_rows], sib)

    ld["up"].wait()
    root = 1.0 / math.sqrt(2.0)
    bell = 1.0 / math.sqrt(2.0 * math.pi)

    def hidden(start):
        r.tmp[...] = nn(r.a3[pl.ds(start, d.RO), :], r.up[...])

        def body(i, c):
            u = r.tmp[pl.ds(i, ROWS), :]
            s = pl.ds(pl.multiple_of(start + i, 16), ROWS)
            half = 0.5 * (1.0 + lax.erf(u * root))
            r.act[s, :] = (u * half).astype(BF)
            slope = half + u * (bell * jnp.exp(-0.5 * u * u))
            r.du[s, :] = (r.dact[s, :] * slope).astype(BF)
            return c

        row_loop(d.RO, body)

    hidden(own)
    a3.wait_recv()
    hidden(other)
    x4 = reduce_rows(4, lambda s: nt(r.du[s, :], r.up[...]))
    for u, lane in (("d1", 0), ("d2", UNIT)):
        units[u].store(tn(r.cot[...], r.act[:, lane : lane + UNIT]), 0)
        units[u].go()
    for u, lane in (("u1", 0), ("u2", UNIT)):
        units[u].store(tn(r.a3[...], r.du[:, lane : lane + UNIT]), 0)
        units[u].go()
    x3 = reduce_rows(3, lambda s: nn(r.act[s, :], r.dn[...]))

    x4.wait_recv()
    gain = vec(r.gain_mlp)
    zero8 = jnp.zeros((8, d.D), F32)

    def back_three(i, c):
        gg, gs = c
        s = pl.ds(i, ROWS)
        e = total(4, s)
        z, inv = normalize(r.h2[s, :])
        dh = r.cot[pl.ds(pl.multiple_of(own + i, 16), ROWS), :].astype(F32) + norm_back(
            z, inv, gain, e
        )
        r.dh[s, :] = dh
        r.c2[s, :] = dh.astype(BF)
        return gg + fold8(e * z), gs + fold8(e)

    gain_mlp_grad, shift_mlp_grad = row_loop(d.RO, back_three, (zero8, zero8))
    r.do2[...] = nt(r.c2[...], r.co[...]).astype(BF)

    def cross_backward(g, c):
        qs = pl.ds(pl.multiple_of(g * d.S, d.S), d.S)
        ks = pl.ds(pl.multiple_of(g * d.K, d.K), d.K)
        for b in range(d.NB):
            lanes = slice(256 * b, 256 * b + 256)
            dp_ = nt(spread(r.do2[qs, lanes], hb2), r.v2[ks, lanes])
            p = r.p2[g * d.NB + b].astype(F32)
            t = p * dp_
            ds = (t - p * jnp.sum(t, axis=-1, keepdims=True)).astype(BF)
            r.ds2[g * d.NB + b] = ds
            r.dq2[qs, lanes] = (gatherh(nn(ds, r.k2[ks, lanes]), hf2) * factor).astype(BF)
        return c

    lax.fori_loop(0, d.GO, cross_backward, 0)
    r.tmp[...] = nn(r.dq2[...], r.cq[...])
    gain = vec(r.gain_cross)

    def back_two(i, c):
        gg, gs = c
        s = pl.ds(i, ROWS)
        e = r.tmp[s, :]
        z, inv = normalize(r.h1[s, :])
        dh = r.dh[s, :] + norm_back(z, inv, gain, e)
        r.dh[s, :] = dh
        r.c1[pl.ds(pl.multiple_of(own + i, 16), ROWS), :] = dh.astype(BF)
        return gg + fold8(e * z), gs + fold8(e)

    gain_cross_grad, shift_cross_grad = row_loop(d.RO, back_two, (zero8, zero8))
    c1 = send(r.c1.at[own_rows], r.c1.at[own_rows], sib)
    steps("d1", "d2")

    r.do1[own_rows, :] = nt(r.c1[own_rows, :], r.so[...]).astype(BF)
    c1.wait_recv()
    r.do1[other_rows, :] = nt(r.c1[other_rows, :], r.so[...]).astype(BF)
    for t in range(d.BLK):
        b = pl.ds(t * 128, 128)
        dom = spread(r.do1[b, :], hb1)
        dp_ = nt(dom, r.v1[b, :])
        pb = r.p1[t]
        p = pb.astype(F32)
        tt = p * dp_
        ds = (tt - p * jnp.sum(tt, axis=-1, keepdims=True)).astype(BF)
        dq = gatherh(nn(ds, r.k1[b, :]), hf1) * factor
        dk = tn(ds, spread(r.q1[b, :], hb1))
        dv = tn(pb, dom)
        r.dqkv[b, : d.C] = dq.astype(BF)
        r.dqkv[b, d.C : 2 * d.C] = dk.astype(BF)
        r.dqkv[b, 2 * d.C :] = dv.astype(BF)
    x6 = reduce_rows(6, lambda s: nn(r.dqkv[s, :], r.wqkv[...]))
    rows = slice(0, d.T)
    units["s1"].store(tn(r.a1[...], r.dqkv[rows, : 2 * d.C]), 0)
    units["s1"].go()
    units["s2"].store(tn(r.a1[...], r.dqkv[rows, 2 * d.C :]), 0)
    units["s2"].store(tn(r.c1[...], r.o1[rows, :]), d.C)
    units["s2"].go()
    steps("u1", "u2", "d1", "d2")

    def cross_keys(g, c):
        qs = pl.ds(pl.multiple_of(g * d.S, d.S), d.S)
        ks = pl.ds(pl.multiple_of(g * d.K, d.K), d.K)
        for b in range(d.NB):
            lanes = slice(256 * b, 256 * b + 256)
            j = g * d.NB + b
            r.k2[ks, lanes] = tn(r.ds2[j], spread(r.q2[qs, lanes], hb2)).astype(BF)
            r.v2[ks, lanes] = tn(r.p2[j], spread(r.do2[qs, lanes], hb2)).astype(BF)
        return c

    lax.fori_loop(0, d.GO, cross_keys, 0)
    pair = pl.ds(pl.multiple_of((mp // 2) * 2 * d.C, 128), 2 * d.C)

    def split_columns(unit, away, lane, value):
        left, right = value[:, : d.C], value[:, d.C :]
        first = core == 0
        unit.store(jnp.where(first, left, right), lane)
        away.store(jnp.where(first, right, left), lane)

    class Away:
        def __init__(self, ref):
            self.acc = ref

        store = Unit.store

    away1, away2 = Away(r.cs1), Away(r.cs2)
    split_columns(units["c1"], away1, 0, tn(r.a2[...], r.dq2[:, pair]))
    split_columns(units["c1"], away1, d.C, tn(r.c2[...], r.o2[:, pair]))
    cc1 = send(r.cs1, r.cr1, sib)
    split_columns(units["c2"], away2, 0, tn(r.mem[...], r.k2[:, pair]))

    def merge(unit, cp, got):
        cp.wait_recv()
        for j in range(d.nch):
            unit.acc[j] = (unit.acc[j].astype(F32) + got[j].astype(F32)).astype(BF)
        unit.go()

    merge(units["c1"], cc1, r.cr1)
    split_columns(units["c2"], away2, d.C, tn(r.mem[...], r.v2[:, pair]))
    cc2 = send(r.cs2, r.cr2, sib)
    steps("u1", "u2")

    x3.wait_recv()

    def finish_out(i, c):
        s = pl.ds(i, ROWS)
        r.layer_out[pl.ds(pl.multiple_of(own + i, 16), ROWS), :] = (r.h2[s, :] + total(3, s)).astype(BF)
        return c

    row_loop(d.RO, finish_out)
    tail = [send(r.layer_out.at[own_rows], r.layer_out.at[own_rows], sib)]
    merge(units["c2"], cc2, r.cr2)

    x6.wait_recv()
    gain = vec(r.gain_self)

    def back_one(i, c):
        gg, gs = c
        s = pl.ds(i, ROWS)
        e = total(6, s)
        z, inv = normalize(r.xin[pl.ds(pl.multiple_of(own + i, 16), ROWS), :].astype(F32))
        r.suffix_grad[pl.ds(pl.multiple_of(own + i, 16), ROWS), :] = (
            r.dh[s, :] + norm_back(z, inv, gain, e)
        ).astype(BF)
        return gg + fold8(e * z), gs + fold8(e)

    gain_self_grad, shift_self_grad = row_loop(d.RO, back_one, (zero8, zero8))
    tail.append(send(r.suffix_grad.at[own_rows], r.suffix_grad.at[own_rows], sib))
    for k, v in enumerate(
        (
            gain_self_grad,
            shift_self_grad,
            gain_cross_grad,
            shift_cross_grad,
            gain_mlp_grad,
            shift_mlp_grad,
        )
    ):
        r.nst[0, k : k + 1, :] = jnp.sum(v, axis=0, keepdims=True)
    r.nst[0, 6:8, :] = jnp.zeros((2, d.D), F32)
    devices = [sib] + [mate(b) for b in range(d.bits)]
    ncp = send(r.nst.at[0], r.nrc.at[0], devices[0])

    def norm_step(k, cp):
        cp.wait_recv()
        r.nst[k + 1] = r.nst[k] + r.nrc[k]
        if k + 1 < len(devices):
            return send(r.nst.at[k + 1], r.nrc.at[k + 1], devices[k + 1])
        return None

    base_r = state["r"]
    state["r"] += d.GO

    def memory_copy(g):
        rows = pl.ds(pl.multiple_of(core * d.MO + g * d.K, 16), d.K)
        return remote(r.memory_grad.at[rows], r.memory_grad.at[rows], sib, base_r + g)

    def memory_group(g, c):
        ks = pl.ds(pl.multiple_of(g * d.K, d.K), d.K)
        value = nn(r.k2[ks, :], r.ck[...]) + nn(r.v2[ks, :], r.cv[...])
        r.memory_grad[pl.ds(pl.multiple_of(core * d.MO + g * d.K, 16), d.K), :] = value.astype(BF)
        memory_copy(g).start()
        return c

    lax.fori_loop(0, d.GO, memory_group, 0)
    ncp = norm_step(0, ncp)
    steps("s1", "s2", "d1", "d2")
    k = 1
    while ncp is not None:
        ncp = norm_step(k, ncp)
        k += 1
        if k == 2:
            steps("c1", "c2")
        if k == 3:
            steps("s1", "s2")
    r.norms[...] = r.nst[len(devices)]
    order = ("d1", "d2", "u1", "u2", "s1", "s2", "c1", "c2")
    while any(units[u].stage < d.bits for u in order):
        for u in order:
            if units[u].stage < d.bits:
                units[u].step()
    for g in range(d.GO):
        memory_copy(g).wait()
    for cp in tail:
        cp.wait_recv()
    for cp in sends:
        cp.wait_send()
    assert state["r"] <= N_SEMS


def solution(mesh):
    n_dp, n_mp = mesh.shape["dp"], mesh.shape["mp"]

    def on_device(*args):
        d = Dims(n_dp, n_mp, args[0], args[1], args[3], args[12], args[20])
        assert d.C * 2 == UNIT and d.F == 2 * UNIT
        scr = scratch(d)
        names = IN_NAMES + OUT_NAMES + tuple(scr)
        col, turned = (d.rp, d.C), (d.C, d.rp)
        shapes = [
            ((d.T, d.D), BF),
            ((d.T, d.D), BF),
            ((d.M, d.D), BF),
            (col, F32),
            (col, F32),
            (col, F32),
            (turned, F32),
            (col, F32),
            (col, F32),
            (col, F32),
            (turned, F32),
            ((d.rp, d.F), F32),
            ((d.rp, d.F), F32),
            ((8, d.D), F32),
        ]
        hbm, vmem = pl.BlockSpec(memory_space=pl.ANY), pl.BlockSpec(memory_space=pltpu.VMEM)
        smem = pl.BlockSpec(memory_space=pltpu.SMEM)

        def body(*refs):
            kernel(d, names, *refs)

        outs = pl.pallas_call(
            body,
            out_shape=[pltpu.VMEM(*s) for s in shapes],
            in_specs=[hbm] * 3 + [smem] * 3 + [vmem] * 6 + [hbm] * 10,
            out_specs=[vmem] * 14,
            scratch_shapes=list(scr.values()),
            compiler_params=pltpu.CompilerParams(
                collective_id=0, has_side_effects=True, vmem_limit_bytes=VMEM_BYTES
            ),
            name="layer",
        )(*(a.T if k in (12, 13, 14, 16, 17, 18) else a for k, a in enumerate(args)))
        outs = [pltpu.with_memory_space_constraint(o, pltpu.VMEM) for o in outs]
        rows = d.D // n_dp

        def write(*refs):
            ins, norms, dst, vectors, sem = refs[:13], refs[13], refs[14:27], refs[27:33], refs[33]
            copies = [
                pltpu.make_async_copy(a, b, sem.at[k]) for k, (a, b) in enumerate(zip(ins, dst))
            ]
            for cp in copies:
                cp.start()
            shift = lax.rem(d.D - lax.axis_index("dp") * rows, d.D)
            mine = pltpu.roll(norms[...], shift, 1)
            for k, v in enumerate(vectors):
                v[...] = mine[k, :rows]
            for cp in copies:
                cp.wait()

        final = pl.pallas_call(
            write,
            out_shape=[jax.ShapeDtypeStruct(*s) for s in shapes[:13]]
            + [jax.ShapeDtypeStruct((rows,), F32)] * 6,
            in_specs=[vmem] * 14,
            out_specs=[hbm] * 13 + [vmem] * 6,
            scratch_shapes=[pltpu.SemaphoreType.DMA((13,))],
            compiler_params=pltpu.CompilerParams(vmem_limit_bytes=2**20),
            name="write",
        )(*outs)
        big, grads, vectors = final[:3], list(final[3:13]), final[13:]
        dp = lax.axis_index("dp")
        if d.low:
            start = lax.rem(dp, 1 << d.low) * rows
            for k, turn in enumerate((0, 0, 0, 1, 0, 0, 0, 1, 0, 0)):
                grads[k] = lax.dynamic_slice_in_dim(grads[k], start, rows, axis=turn)
        grads[9] = grads[9].T
        return (*big, *grads, *vectors)

    row, col, turn = P("dp", None), P("dp", "mp"), P("mp", "dp")
    wide, tall = P(None, "mp"), P("mp", None)
    in_specs = (row,) * 3 + (P("dp"),) * 3 + (P(),) * 6
    in_specs += (wide, wide, wide, tall, wide, wide, wide, tall, wide, tall)
    out_specs = (row,) * 3 + (col, col, col, turn, col, col, col, turn, col, turn)
    out_specs += (P("dp"),) * 6
    return jax.shard_map(
        on_device, mesh=mesh, in_specs=in_specs, out_specs=out_specs, check_vma=False
    )
```

```python
import math

import jax
import jax.numpy as jnp
from jax import lax
from jax.experimental import pallas as pl
from jax.experimental.pallas import tpu as pltpu
from jax.sharding import PartitionSpec as P

BF = jnp.bfloat16
F32 = jnp.float32
MESH = pl.DeviceIdType.MESH
HEAD = 64
PATCHES = 196
EPSILON = 1e-06
NEG_FILL = -1e30
UNIT = 384
ROWS = 112
N_SEMS = 160
VMEM_BYTES = 54 * 2**20


def nn(a, b):
    return lax.dot_general(a, b, (((1,), (0,)), ((), ())), preferred_element_type=F32)


def nt(a, b):
    return lax.dot_general(a, b, (((1,), (1,)), ((), ())), preferred_element_type=F32)


def tn(a, b):
    return lax.dot_general(a, b, (((0,), (0,)), ((), ())), preferred_element_type=F32)


def normalize(v):
    centred = v - jnp.mean(v, axis=-1, keepdims=True)
    inverse = lax.rsqrt(jnp.mean(centred * centred, axis=-1, keepdims=True) + EPSILON)
    return centred * inverse, inverse


def norm_back(unit, inverse, gain, incoming):
    w = incoming * gain
    return inverse * (
        w - jnp.mean(w, axis=-1, keepdims=True) - unit * jnp.mean(w * unit, axis=-1, keepdims=True)
    )


def softmax(s):
    p = jnp.exp(s - jnp.max(s, axis=-1, keepdims=True))
    return p * (1.0 / jnp.sum(p, axis=-1, keepdims=True))


def fold8(v):
    total = v[0:8]
    for k in range(8, v.shape[0], 8):
        total = total + v[k : k + 8]
    return total


class Dims:
    def __init__(self, n_dp, n_mp, suffix, memory, group_kind, self_query, mlp_up):
        assert n_mp == 4
        self.n_dp = n_dp
        self.T, self.D = suffix.shape
        self.M = memory.shape[0]
        self.G = group_kind.shape[0]
        self.C = self_query.shape[1]
        self.F = mlp_up.shape[1]
        self.H = n_mp * self.C
        self.S = self.T // self.G
        self.K = self.M // self.G
        self.GO, self.RO, self.MO = self.G // 2, self.T // 2, self.M // 2
        self.NB = self.H // 256
        self.BLK = pl.cdiv(self.T, 128)
        self.TP = self.BLK * 128
        self.bits = n_dp.bit_length() - 1
        assert 1 << self.bits == n_dp and n_dp >= 4
        halvings = 0
        while halvings < self.bits and (self.D >> (halvings + 1)) % 16 == 0:
            halvings += 1
        self.halvings = halvings
        self.low = self.bits - halvings
        self.nch = 1 << halvings
        self.rp = self.D // self.nch


UNITS = ("d1", "d2", "u1", "u2", "s1", "s2", "c1", "c2")
IN_NAMES = (
    "suffix",
    "memory",
    "cotangent",
    "kind",
    "prefix",
    "slen",
    "gain_self",
    "shift_self",
    "gain_cross",
    "shift_cross",
    "gain_mlp",
    "shift_mlp",
    "self_query",
    "self_key",
    "self_value",
    "self_out",
    "cross_query",
    "cross_key",
    "cross_value",
    "cross_out",
    "mlp_up",
    "mlp_down",
)
OUT_NAMES = (
    "layer_out",
    "suffix_grad",
    "memory_grad",
    "g_sq",
    "g_sk",
    "g_sv",
    "g_so",
    "g_cq",
    "g_ck",
    "g_cv",
    "g_co",
    "g_up",
    "g_dn",
    "norms",
)


def scratch(d):
    s = {}
    T, D, C, F, H, RO, MO, K = d.T, d.D, d.C, d.F, d.H, d.RO, d.MO, d.K

    def vmem(name, shape, dtype=BF):
        s[name] = pltpu.VMEM(shape, dtype)

    vmem("xin", (T, D))
    vmem("cot", (T, D))
    vmem("mem", (MO, D))
    vmem("wqkv", (3 * C, D))
    vmem("so", (C, D))
    for n in ("cq", "ck", "cv", "co"):
        vmem(n, (H, D))
    vmem("up", (D, F))
    vmem("dn", (F, D))
    vmem("a1", (T, D))
    for n in ("q1", "k1", "v1", "o1", "do1"):
        vmem(n, (d.TP, C))
    vmem("p1", (d.BLK, 3 * 128, 128))
    vmem("dqkv", (d.TP, 3 * C))
    for k in (1, 3, 4, 6):
        for n in ("s", "r", "xs", "xr"):
            vmem(f"{n}{k}", (RO, D))
    vmem("h1", (RO, D), F32)
    vmem("h2", (RO, D), F32)
    vmem("dh", (RO, D), F32)
    vmem("tmp", (RO, D), F32)
    vmem("a2", (RO, D))
    vmem("c2", (RO, D))
    for n in ("q2", "o2", "do2", "dq2"):
        vmem(n, (RO, H))
    for n in ("k2", "v2"):
        vmem(n, (MO, H))
    for n in ("p2", "ds2"):
        vmem(n, (d.GO * d.NB, 4 * d.S, K))
    vmem("a3", (T, D))
    vmem("c1", (T, D))
    vmem("act", (T, F))
    vmem("du", (T, F))
    vmem("dact", (T, F), F32)
    for n in ("cs1", "cs2", "cr1", "cr2"):
        vmem(n, (d.nch, d.rp, UNIT))
    for u in UNITS:
        vmem("g_" + u + "_acc", (d.nch, d.rp, UNIT))
        for k in range(d.halvings):
            vmem(f"g_{u}_r{k}", (d.nch >> (k + 1), d.rp, UNIT))
        for k in range(d.low):
            vmem(f"g_{u}_x{k}", (d.rp, UNIT))
            vmem(f"g_{u}_y{k}", (d.rp, UNIT))
    vmem("nst", (2 + d.bits, 8, D), F32)
    vmem("nrc", (1 + d.bits, 8, D), F32)
    s["ss"] = pltpu.SemaphoreType.DMA((N_SEMS,))
    s["rs"] = pltpu.SemaphoreType.DMA((N_SEMS,))
    s["ls"] = pltpu.SemaphoreType.DMA((48,))
    return s


class Refs:
    pass


def kernel(d, names, *args):
    r = Refs()
    for name, ref in zip(names, args):
        setattr(r, name, ref)
    dp, mp = lax.axis_index("dp"), lax.axis_index("mp")
    core = lax.rem(mp, 2)
    sib = {"mp": mp + 1 - 2 * core}
    xmate = {"mp": lax.rem(mp + 2, 4)}
    own = pl.multiple_of(core * d.RO, 16)
    other = pl.multiple_of((1 - core) * d.RO, 16)
    own_rows, other_rows = pl.ds(own, d.RO), pl.ds(other, d.RO)
    factor = 1.0 / math.sqrt(HEAD)

    def bit_of(b):
        return lax.rem(dp // (1 << b), 2)

    def mate(b):
        return {"dp": dp + (1 << b) * (1 - 2 * bit_of(b))}

    corner = {"dp": dp + 3 - 2 * bit_of(0) - 4 * bit_of(1)}

    state = {"r": 0, "l": 0}
    sends = []

    def remote(src, dst, device, index=None):
        if index is None:
            index = state["r"]
            state["r"] += 1
        cp = pltpu.make_async_remote_copy(
            src_ref=src,
            dst_ref=dst,
            send_sem=r.ss.at[index],
            recv_sem=r.rs.at[index],
            device_id=device,
            device_id_type=MESH,
        )
        return cp

    def send(src, dst, device):
        cp = remote(src, dst, device)
        cp.start()
        sends.append(cp)
        return cp

    def load(src, dst):
        cp = pltpu.make_async_copy(src, dst, r.ls.at[state["l"]])
        state["l"] += 1
        cp.start()
        return cp

    ld = {}
    mp_rows = pl.ds(pl.multiple_of(mp * d.C, 16), d.C)
    ld["ck"] = load(r.cross_key, r.ck.at[mp_rows])
    ld["cv"] = load(r.cross_value, r.cv.at[mp_rows])
    ld["cq"] = load(r.cross_query, r.cq.at[mp_rows])
    ld["co"] = load(r.cross_out, r.co.at[mp_rows])
    ld["xin"] = load(r.suffix, r.xin)
    ld["sq"] = load(r.self_query, r.wqkv.at[pl.ds(0, d.C)])
    ld["sk"] = load(r.self_key, r.wqkv.at[pl.ds(d.C, d.C)])
    ld["sv"] = load(r.self_value, r.wqkv.at[pl.ds(2 * d.C, d.C)])
    ld["so"] = load(r.self_out, r.so)
    ld["cot"] = load(r.cotangent, r.cot)
    ld["dn"] = load(r.mlp_down, r.dn)
    ld["mem"] = load(r.memory.at[pl.ds(pl.multiple_of(core * d.MO, 16), d.MO)], r.mem)
    ld["up"] = load(r.mlp_up, r.up)

    barrier = pltpu.get_barrier_semaphore()
    mates = [sib, xmate, corner] + [mate(b) for b in range(d.bits)]
    for device in mates:
        pl.semaphore_signal(barrier, inc=1, device_id=device, device_id_type=MESH)
    pl.semaphore_wait(barrier, len(mates))

    PC = d.C // 4
    piece = lax.rem(dp, 4)
    full = {"ck": r.ck, "cv": r.cv, "cq": r.cq, "co": r.co}
    xm = lax.rem(mp + 2, 4)
    xm_rows = pl.ds(pl.multiple_of(xm * d.C, 16), d.C)
    gat = {}

    def part(ref, owner, which):
        return ref.at[pl.ds(pl.multiple_of(owner * d.C + which * PC, 16), PC)]

    def gather_start(w):
        ref = full[w]
        ld[w].wait()
        mine = part(ref, mp, piece)
        gat[w, "x"] = send(mine, mine, xmate)
        gat[w, "s"] = send(ref.at[mp_rows], ref.at[mp_rows], sib)

    def gather_x(w):
        gat[w, "x"].wait_recv()
        got = part(full[w], xm, piece)
        for k, device in enumerate((mate(0), mate(1), corner)):
            gat[w, k] = send(got, got, device)

    def gather_y(w):
        for k in range(3):
            gat[w, k].wait_recv()
        gat[w, "f"] = send(full[w].at[xm_rows], full[w].at[xm_rows], sib)

    def gather_done(w):
        gat[w, "s"].wait_recv()
        gat[w, "f"].wait_recv()

    for w in ("ck", "cv", "cq", "co"):
        gather_start(w)

    class Unit:
        def __init__(self, name, finish, swap=False):
            self.name, self.finish, self.stage = name, finish, 0
            self.order = list(range(d.halvings))
            if swap:
                self.order[:2] = 1, 0
            self.acc = getattr(r, f"g_{name}_acc")
            self.base = 0
            self.cp = None

        def store(self, value, lane):
            width = value.shape[1]
            for j in range(d.nch):
                p = sum(((j >> b) & 1) * (d.nch >> (k + 1)) for k, b in enumerate(self.order))
                self.acc[p, :, lane : lane + width] = value[j * d.rp : (j + 1) * d.rp].astype(BF)

        def go(self):
            k = self.stage
            if k < d.halvings:
                half = d.nch >> (k + 1)
                b = d.low + self.order[k]
                dst = getattr(r, f"g_{self.name}_r{k}")
                src = self.acc.at[pl.ds(self.base + (1 - bit_of(b)) * half, half)]
                self.cp = send(src, dst, mate(b))
            else:
                e = k - d.halvings
                x = getattr(r, f"g_{self.name}_x{e}")
                x[...] = self.value.astype(BF)
                self.cp = send(x, getattr(r, f"g_{self.name}_y{e}"), mate(e))

        def step(self):
            k = self.stage
            self.cp.wait_recv()
            if k < d.halvings:
                half = d.nch >> (k + 1)
                got = getattr(r, f"g_{self.name}_r{k}")
                base = self.base + bit_of(d.low + self.order[k]) * half
                self.base = base
                if k < d.halvings - 1:
                    for j in range(half):
                        self.acc[base + j] = (
                            self.acc[base + j].astype(F32) + got[j].astype(F32)
                        ).astype(BF)
                else:
                    self.value = self.acc[base].astype(F32) + got[0].astype(F32)
            else:
                e = k - d.halvings
                x = getattr(r, f"g_{self.name}_x{e}")
                y = getattr(r, f"g_{self.name}_y{e}")
                self.value = x[...].astype(F32) + y[...].astype(F32)
            self.stage += 1
            if self.stage < d.bits:
                self.go()
            else:
                self.finish(self.value)

        def drain(self):
            while self.stage < d.bits:
                self.step()

    def fin_dn(lane):
        def f(v):
            r.g_dn[:, lane : lane + UNIT] = v

        return f

    def fin_up(lane):
        def f(v):
            r.g_up[:, lane : lane + UNIT] = v

        return f

    def fin_pair(left, right, turn):
        def f(v):
            left[...] = v[:, : d.C]
            right[...] = v[:, d.C :].T if turn else v[:, d.C :]

        return f

    units = {
        "d1": Unit("d1", fin_dn(0)),
        "d2": Unit("d2", fin_dn(UNIT), True),
        "u1": Unit("u1", fin_up(0)),
        "u2": Unit("u2", fin_up(UNIT)),
        "s1": Unit("s1", fin_pair(r.g_sq, r.g_sk, False)),
        "s2": Unit("s2", fin_pair(r.g_sv, r.g_so, True), True),
        "c1": Unit("c1", fin_pair(r.g_cq, r.g_co, True)),
        "c2": Unit("c2", fin_pair(r.g_ck, r.g_cv, False)),
    }

    def steps(*which):
        for u in which:
            if units[u].stage < d.bits:
                units[u].step()

    def reduce_begin(k, partial):
        getattr(r, f"s{k}")[...] = partial(other_rows).astype(BF)
        return send(getattr(r, f"s{k}"), getattr(r, f"r{k}"), sib)

    def reduce_end(k, partial, cp):
        got, xs, xr = (getattr(r, f"{n}{k}") for n in ("r", "xs", "xr"))
        value = partial(own_rows)
        cp.wait_recv()
        xs[...] = (value + got[...].astype(F32)).astype(BF)
        return send(xs, xr, xmate)

    def total(k, s):
        return getattr(r, f"xs{k}")[s, :].astype(F32) + getattr(r, f"xr{k}")[s, :].astype(F32)

    def row_loop(n, body, carry=0):
        def step(i, c):
            return body(pl.multiple_of(i * ROWS, ROWS), c)

        return lax.fori_loop(0, n // ROWS, step, carry)

    def vec(ref):
        return ref[...].reshape(1, d.D)

    def head_masks(width, count):
        col = lax.broadcasted_iota(jnp.int32, (1, width), 1)
        f = [((col >= HEAD * h) & (col < HEAD * h + HEAD)).astype(F32) for h in range(count)]
        return f, [m.astype(BF) for m in f]

    HC = d.C // HEAD
    hf1, hb1 = head_masks(d.C, HC)
    hf2, hb2 = head_masks(256, 4)

    def spread(v, masks):
        return jnp.concatenate([v * m for m in masks], axis=0)

    def gatherh(v, masks):
        n = v.shape[0] // len(masks)
        out = v[:n] * masks[0]
        for h in range(1, len(masks)):
            out = out + v[h * n : (h + 1) * n] * masks[h]
        return out

    for n in ("q1", "k1", "v1", "o1", "do1"):
        ref = getattr(r, n)
        ref[d.T :, :] = jnp.zeros((d.TP - d.T, d.C), BF)
    ld["xin"].wait()
    gain, shift = vec(r.gain_self), vec(r.shift_self)

    def norm_one(i, c):
        s = pl.ds(i, ROWS)
        z, _ = normalize(r.xin[s, :].astype(F32))
        r.a1[s, :] = (z * gain + shift).astype(BF)
        return c

    row_loop(d.T, norm_one)
    for n in ("sq", "sk", "sv"):
        ld[n].wait()
    qkv = nt(r.a1[...], r.wqkv[...])
    r.q1[: d.T, :] = (qkv[:, : d.C] * factor).astype(BF)
    r.k1[: d.T, :] = qkv[:, d.C : 2 * d.C].astype(BF)
    r.v1[: d.T, :] = qkv[:, 2 * d.C :].astype(BF)
    gather_x("ck")

    ri = lax.broadcasted_iota(jnp.int32, (128, 128), 0)
    ci = lax.broadcasted_iota(jnp.int32, (128, 128), 1)
    near = (jnp.right_shift(ri, 5) == jnp.right_shift(ci, 5)) & (ci <= ri)
    place = jnp.bitwise_and(ci, 31)
    per = 128 // d.S
    for t in range(d.BLK):
        lens = jnp.zeros((128, 128), jnp.int32)
        for k in range(per):
            g = t * per + k
            if g < d.G:
                lens = jnp.where(jnp.right_shift(ci, 5) == k, r.slen[g], lens)
        ok = near & (place < lens)
        b = pl.ds(t * 128, 128)
        scores = nt(spread(r.q1[b, :], hb1), r.k1[b, :])
        scores = jnp.concatenate(
            [jnp.where(ok, scores[h * 128 : (h + 1) * 128], NEG_FILL) for h in range(HC)], axis=0
        )
        p = softmax(scores).astype(BF)
        r.p1[t] = p
        r.o1[b, :] = gatherh(nn(p, r.v1[b, :]), hf1).astype(BF)
    gather_x("cv")
    ld["so"].wait()

    def out_one(rows):
        return nn(r.o1[rows, :], r.so[...])

    x1 = reduce_begin(1, out_one)
    ld["cot"].wait()
    ld["dn"].wait()
    r.dact[...] = nt(r.cot[...], r.dn[...])
    x1 = reduce_end(1, out_one, x1)

    gather_x("cq")
    gather_x("co")
    gather_y("ck")
    ld["mem"].wait()
    big = d.MO // 2

    def project(w, dst):
        def body(i, c):
            s = pl.ds(pl.multiple_of(i * big, 16), big)
            dst[s, :] = nt(r.mem[s, :], w[...]).astype(BF)
            return c

        lax.fori_loop(0, 2, body, 0)

    gather_done("ck")
    project(r.ck, r.k2)
    gather_y("cv")
    gather_done("cv")
    project(r.cv, r.v2)
    gather_y("cq")

    x1.wait_recv()
    gain, shift = vec(r.gain_cross), vec(r.shift_cross)

    def norm_two(i, c):
        s = pl.ds(i, ROWS)
        h1 = r.xin[pl.ds(pl.multiple_of(own + i, 16), ROWS), :].astype(F32) + total(1, s)
        r.h1[s, :] = h1
        z, _ = normalize(h1)
        r.a2[s, :] = (z * gain + shift).astype(BF)
        return c

    row_loop(d.RO, norm_two)
    gather_done("cq")
    r.q2[...] = (nt(r.a2[...], r.cq[...]) * factor).astype(BF)
    slot = lax.broadcasted_iota(jnp.int32, (4 * d.S, d.K), 1)

    blocks = [slice(256 * b, 256 * b + 256) for b in range(d.NB)]

    def cross_forward(g, c):
        n = core * d.GO + g
        live = r.kind[n] * PATCHES + r.prefix[n]
        qs = pl.ds(pl.multiple_of(g * d.S, d.S), d.S)
        ks = pl.ds(pl.multiple_of(g * d.K, d.K), d.K)
        v = [r.v2[ks, b] for b in blocks]
        s = [nt(spread(r.q2[qs, b], hb2), r.k2[ks, b]) for b in blocks]
        s = [jnp.where(slot < live, x, NEG_FILL) for x in s]
        top = [jnp.max(x, axis=-1, keepdims=True) for x in s]
        p = [jnp.exp(x - t) for x, t in zip(s, top)]
        scale = [1.0 / jnp.sum(x, axis=-1, keepdims=True) for x in p]
        p = [(x * t).astype(BF) for x, t in zip(p, scale)]
        o = [nn(x, y) for x, y in zip(p, v)]
        o = [gatherh(x, hf2).astype(BF) for x in o]
        for k, b in enumerate(blocks):
            r.p2[g * d.NB + k] = p[k]
            r.o2[qs, b] = o[k]
        return c

    lax.fori_loop(0, d.GO, cross_forward, 0)
    gather_y("co")
    gather_done("co")
    r.tmp[...] = nn(r.o2[...], r.co[...])
    gain, shift = vec(r.gain_mlp), vec(r.shift_mlp)

    def norm_three(i, c):
        s = pl.ds(i, ROWS)
        h2 = r.h1[s, :] + r.tmp[s, :]
        r.h2[s, :] = h2
        z, _ = normalize(h2)
        r.a3[pl.ds(pl.multiple_of(own + i, 16), ROWS), :] = (z * gain + shift).astype(BF)
        return c

    row_loop(d.RO, norm_three)
    a3 = send(r.a3.at[own_rows], r.a3.at[own_rows], sib)

    ld["up"].wait()
    root = 1.0 / math.sqrt(2.0)
    bell = 1.0 / math.sqrt(2.0 * math.pi)

    def hidden(start):
        r.tmp[...] = nn(r.a3[pl.ds(start, d.RO), :], r.up[...])

        def body(i, c):
            u = r.tmp[pl.ds(i, ROWS), :]
            s = pl.ds(pl.multiple_of(start + i, 16), ROWS)
            half = 0.5 * (1.0 + lax.erf(u * root))
            r.act[s, :] = (u * half).astype(BF)
            slope = half + u * (bell * jnp.exp(-0.5 * u * u))
            r.du[s, :] = (r.dact[s, :] * slope).astype(BF)
            return c

        row_loop(d.RO, body)

    hidden(own)
    a3.wait_recv()
    hidden(other)

    def back_four(rows):
        return nt(r.du[rows, :], r.up[...])

    def out_three(rows):
        return nn(r.act[rows, :], r.dn[...])

    x4 = reduce_begin(4, back_four)
    for u, lane in (("d1", 0), ("d2", UNIT)):
        units[u].store(tn(r.cot[...], r.act[:, lane : lane + UNIT]), 0)
        units[u].go()
    x4 = reduce_end(4, back_four, x4)
    x3 = reduce_begin(3, out_three)
    for u, lane in (("u1", 0), ("u2", UNIT)):
        units[u].store(tn(r.a3[...], r.du[:, lane : lane + UNIT]), 0)
        units[u].go()
    x3 = reduce_end(3, out_three, x3)

    x4.wait_recv()
    gain = vec(r.gain_mlp)
    zero8 = jnp.zeros((8, d.D), F32)

    def back_three(i, c):
        gg, gs = c
        s = pl.ds(i, ROWS)
        e = total(4, s)
        z, inv = normalize(r.h2[s, :])
        dh = r.cot[pl.ds(pl.multiple_of(own + i, 16), ROWS), :].astype(F32) + norm_back(
            z, inv, gain, e
        )
        r.dh[s, :] = dh
        r.c2[s, :] = dh.astype(BF)
        return gg + fold8(e * z), gs + fold8(e)

    gain_mlp_grad, shift_mlp_grad = row_loop(d.RO, back_three, (zero8, zero8))
    r.do2[...] = nt(r.c2[...], r.co[...]).astype(BF)

    def cross_backward(g, c):
        qs = pl.ds(pl.multiple_of(g * d.S, d.S), d.S)
        ks = pl.ds(pl.multiple_of(g * d.K, d.K), d.K)
        k2 = [r.k2[ks, b] for b in blocks]
        p = [r.p2[g * d.NB + k].astype(F32) for k in range(d.NB)]
        t = [nt(spread(r.do2[qs, b], hb2), r.v2[ks, b]) for b in blocks]
        t = [x * y for x, y in zip(p, t)]
        centre = [jnp.sum(x, axis=-1, keepdims=True) for x in t]
        ds = [(x - y * m).astype(BF) for x, y, m in zip(t, p, centre)]
        dq = [nn(x, y) for x, y in zip(ds, k2)]
        dq = [(gatherh(x, hf2) * factor).astype(BF) for x in dq]
        for k, b in enumerate(blocks):
            r.ds2[g * d.NB + k] = ds[k]
            r.dq2[qs, b] = dq[k]
        return c

    steps("d1", "d2")
    lax.fori_loop(0, d.GO, cross_backward, 0)
    r.tmp[...] = nn(r.dq2[...], r.cq[...])
    steps("u1")
    gain = vec(r.gain_cross)

    def back_two(i, c):
        gg, gs = c
        s = pl.ds(i, ROWS)
        e = r.tmp[s, :]
        z, inv = normalize(r.h1[s, :])
        dh = r.dh[s, :] + norm_back(z, inv, gain, e)
        r.dh[s, :] = dh
        r.c1[pl.ds(pl.multiple_of(own + i, 16), ROWS), :] = dh.astype(BF)
        return gg + fold8(e * z), gs + fold8(e)

    gain_cross_grad, shift_cross_grad = row_loop(d.RO, back_two, (zero8, zero8))
    c1 = send(r.c1.at[own_rows], r.c1.at[own_rows], sib)
    pair = pl.ds(pl.multiple_of((mp // 2) * 2 * d.C, 128), 2 * d.C)

    def split_columns(unit, away, lane, value):
        left, right = value[:, : d.C], value[:, d.C :]
        first = core == 0
        unit.store(jnp.where(first, left, right), lane)
        away.store(jnp.where(first, right, left), lane)

    class Away:
        def __init__(self, ref, order):
            self.acc, self.order = ref, order

        store = Unit.store

    away1 = Away(r.cs1, units["c1"].order)
    away2 = Away(r.cs2, units["c2"].order)
    def merge(unit, cp, got):
        cp.wait_recv()
        for j in range(d.nch):
            unit.acc[j] = (unit.acc[j].astype(F32) + got[j].astype(F32)).astype(BF)
        unit.go()

    split_columns(units["c1"], away1, 0, tn(r.a2[...], r.dq2[:, pair]))
    split_columns(units["c1"], away1, d.C, tn(r.c2[...], r.o2[:, pair]))
    cc1 = send(r.cs1, r.cr1, sib)
    r.do1[own_rows, :] = nt(r.c1[own_rows, :], r.so[...]).astype(BF)
    c1.wait_recv()
    r.do1[other_rows, :] = nt(r.c1[other_rows, :], r.so[...]).astype(BF)
    for t in range(d.BLK):
        b = pl.ds(t * 128, 128)
        dom = spread(r.do1[b, :], hb1)
        dp_ = nt(dom, r.v1[b, :])
        pb = r.p1[t]
        p = pb.astype(F32)
        tt = p * dp_
        ds = (tt - p * jnp.sum(tt, axis=-1, keepdims=True)).astype(BF)
        dq = gatherh(nn(ds, r.k1[b, :]), hf1) * factor
        dk = tn(ds, spread(r.q1[b, :], hb1))
        dv = tn(pb, dom)
        r.dqkv[b, : d.C] = dq.astype(BF)
        r.dqkv[b, d.C : 2 * d.C] = dk.astype(BF)
        r.dqkv[b, 2 * d.C :] = dv.astype(BF)
    steps("d1", "d2")

    def back_six(rows):
        return nn(r.dqkv[rows, :], r.wqkv[...])

    rows = slice(0, d.T)
    x6 = reduce_begin(6, back_six)
    units["s1"].store(tn(r.a1[...], r.dqkv[rows, : 2 * d.C]), 0)
    units["s1"].go()
    x6 = reduce_end(6, back_six, x6)
    units["s2"].store(tn(r.a1[...], r.dqkv[rows, 2 * d.C :]), 0)
    units["s2"].store(tn(r.c1[...], r.o1[rows, :]), d.C)
    units["s2"].go()
    merge(units["c1"], cc1, r.cr1)
    steps("u2", "u1")

    def cross_keys(g, c):
        qs = pl.ds(pl.multiple_of(g * d.S, d.S), d.S)
        ks = pl.ds(pl.multiple_of(g * d.K, d.K), d.K)
        j = g * d.NB
        dk = [tn(r.ds2[j + k], spread(r.q2[qs, b], hb2)).astype(BF) for k, b in enumerate(blocks)]
        dv = [tn(r.p2[j + k], spread(r.do2[qs, b], hb2)).astype(BF) for k, b in enumerate(blocks)]
        for k, b in enumerate(blocks):
            r.k2[ks, b] = dk[k]
            r.v2[ks, b] = dv[k]
        return c

    lax.fori_loop(0, d.GO, cross_keys, 0)
    split_columns(units["c2"], away2, 0, tn(r.mem[...], r.k2[:, pair]))
    split_columns(units["c2"], away2, d.C, tn(r.mem[...], r.v2[:, pair]))
    cc2 = send(r.cs2, r.cr2, sib)
    steps("d1", "d2")
    x3.wait_recv()

    def finish_out(i, c):
        s = pl.ds(i, ROWS)
        r.layer_out[pl.ds(pl.multiple_of(own + i, 16), ROWS), :] = (r.h2[s, :] + total(3, s)).astype(BF)
        return c

    row_loop(d.RO, finish_out)
    tail = [send(r.layer_out.at[own_rows], r.layer_out.at[own_rows], sib)]
    merge(units["c2"], cc2, r.cr2)

    x6.wait_recv()
    gain = vec(r.gain_self)

    def back_one(i, c):
        gg, gs = c
        s = pl.ds(i, ROWS)
        e = total(6, s)
        z, inv = normalize(r.xin[pl.ds(pl.multiple_of(own + i, 16), ROWS), :].astype(F32))
        r.suffix_grad[pl.ds(pl.multiple_of(own + i, 16), ROWS), :] = (
            r.dh[s, :] + norm_back(z, inv, gain, e)
        ).astype(BF)
        return gg + fold8(e * z), gs + fold8(e)

    gain_self_grad, shift_self_grad = row_loop(d.RO, back_one, (zero8, zero8))
    tail.append(send(r.suffix_grad.at[own_rows], r.suffix_grad.at[own_rows], sib))
    for k, v in enumerate(
        (
            gain_self_grad,
            shift_self_grad,
            gain_cross_grad,
            shift_cross_grad,
            gain_mlp_grad,
            shift_mlp_grad,
        )
    ):
        r.nst[0, k : k + 1, :] = jnp.sum(v, axis=0, keepdims=True)
    r.nst[0, 6:8, :] = jnp.zeros((2, d.D), F32)
    devices = [sib] + [mate(b) for b in range(d.bits)]
    ncp = send(r.nst.at[0], r.nrc.at[0], devices[0])

    def norm_step(k, cp):
        cp.wait_recv()
        r.nst[k + 1] = r.nst[k] + r.nrc[k]
        if k + 1 < len(devices):
            return send(r.nst.at[k + 1], r.nrc.at[k + 1], devices[k + 1])
        return None

    parts = 4
    base_r = state["r"]
    state["r"] += parts
    piece_rows = d.MO // parts

    def memory_copy(i):
        rows = pl.ds(pl.multiple_of(core * d.MO + i * piece_rows, 16), piece_rows)
        return remote(r.memory_grad.at[rows], r.memory_grad.at[rows], sib, base_r + i)

    def memory_part(i, c):
        s = pl.ds(pl.multiple_of(i * piece_rows, 16), piece_rows)
        there = pl.ds(pl.multiple_of(core * d.MO + i * piece_rows, 16), piece_rows)
        value = nn(r.k2[s, :], r.ck[...]) + nn(r.v2[s, :], r.cv[...])
        r.memory_grad[there, :] = value.astype(BF)
        memory_copy(i).start()
        return c

    lax.fori_loop(0, 2, memory_part, 0)
    ncp = norm_step(0, ncp)
    steps("s1", "u2", "c1", "u1")
    lax.fori_loop(2, 4, memory_part, 0)
    k = 1
    rounds = [("s2", "u2"), ("c1", "s1"), ("c2", "s2")]
    while ncp is not None:
        ncp = norm_step(k, ncp)
        if rounds:
            steps(*rounds.pop(0))
        k += 1
    r.norms[...] = r.nst[len(devices)]
    order = ("d1", "d2", "u1", "u2", "s1", "c1", "s2", "c2")
    while any(units[u].stage < d.bits for u in order):
        for u in order:
            if units[u].stage < d.bits:
                units[u].step()
    for i in range(parts):
        memory_copy(i).wait()
    for cp in tail:
        cp.wait_recv()
    for cp in sends:
        cp.wait_send()
    assert state["r"] <= N_SEMS


def solution(mesh):
    n_dp, n_mp = mesh.shape["dp"], mesh.shape["mp"]

    def on_device(*args):
        d = Dims(n_dp, n_mp, args[0], args[1], args[3], args[12], args[20])
        assert d.C * 2 == UNIT and d.F == 2 * UNIT
        scr = scratch(d)
        names = IN_NAMES + OUT_NAMES + tuple(scr)
        col, turned = (d.rp, d.C), (d.C, d.rp)
        shapes = [
            ((d.T, d.D), BF),
            ((d.T, d.D), BF),
            ((d.M, d.D), BF),
            (col, F32),
            (col, F32),
            (col, F32),
            (turned, F32),
            (col, F32),
            (col, F32),
            (col, F32),
            (turned, F32),
            ((d.rp, d.F), F32),
            ((d.rp, d.F), F32),
            ((8, d.D), F32),
        ]
        hbm, vmem = pl.BlockSpec(memory_space=pl.ANY), pl.BlockSpec(memory_space=pltpu.VMEM)
        smem = pl.BlockSpec(memory_space=pltpu.SMEM)

        def body(*refs):
            kernel(d, names, *refs)

        outs = pl.pallas_call(
            body,
            out_shape=[pltpu.VMEM(*s) for s in shapes],
            in_specs=[hbm] * 3 + [smem] * 3 + [vmem] * 6 + [hbm] * 10,
            out_specs=[vmem] * 14,
            scratch_shapes=list(scr.values()),
            compiler_params=pltpu.CompilerParams(
                collective_id=0, has_side_effects=True, vmem_limit_bytes=VMEM_BYTES
            ),
            name="layer",
        )(*(a.T if k in (12, 13, 14, 16, 17, 18) else a for k, a in enumerate(args)))
        outs = [pltpu.with_memory_space_constraint(o, pltpu.VMEM) for o in outs]
        rows = d.D // n_dp

        def write(*refs):
            ins, norms, dst, vectors, sem = refs[:13], refs[13], refs[14:27], refs[27:33], refs[33]
            copies = [
                pltpu.make_async_copy(a, b, sem.at[k]) for k, (a, b) in enumerate(zip(ins, dst))
            ]
            for cp in copies:
                cp.start()
            shift = lax.rem(d.D - lax.axis_index("dp") * rows, d.D)
            mine = pltpu.roll(norms[...], shift, 1)
            for k, v in enumerate(vectors):
                v[...] = mine[k, :rows]
            for cp in copies:
                cp.wait()

        final = pl.pallas_call(
            write,
            out_shape=[jax.ShapeDtypeStruct(*s) for s in shapes[:13]]
            + [jax.ShapeDtypeStruct((rows,), F32)] * 6,
            in_specs=[vmem] * 14,
            out_specs=[hbm] * 13 + [vmem] * 6,
            scratch_shapes=[pltpu.SemaphoreType.DMA((13,))],
            compiler_params=pltpu.CompilerParams(vmem_limit_bytes=2**20),
            name="write",
        )(*outs)
        big, grads, vectors = final[:3], list(final[3:13]), final[13:]
        dp = lax.axis_index("dp")
        if d.low:
            start = lax.rem(dp, 1 << d.low) * rows
            for k, turn in enumerate((0, 0, 0, 1, 0, 0, 0, 1, 0, 0)):
                grads[k] = lax.dynamic_slice_in_dim(grads[k], start, rows, axis=turn)
        grads[9] = grads[9].T
        return (*big, *grads, *vectors)

    row, col, turn = P("dp", None), P("dp", "mp"), P("mp", "dp")
    wide, tall = P(None, "mp"), P("mp", None)
    in_specs = (row,) * 3 + (P("dp"),) * 3 + (P(),) * 6
    in_specs += (wide, wide, wide, tall, wide, wide, wide, tall, wide, tall)
    out_specs = (row,) * 3 + (col, col, col, turn, col, col, col, turn, col, turn)
    out_specs += (P("dp"),) * 6
    return jax.shard_map(
        on_device, mesh=mesh, in_specs=in_specs, out_specs=out_specs, check_vma=False
    )
```

```python
import math

import jax
import jax.numpy as jnp
from jax import lax
from jax.experimental import pallas as pl
from jax.experimental.pallas import tpu as pltpu
from jax.sharding import PartitionSpec as P

BF = jnp.bfloat16
F32 = jnp.float32
MESH = pl.DeviceIdType.MESH
HEAD = 64
PATCHES = 196
EPSILON = 1e-06
NEG_FILL = -1e30
UNIT = 384
GP = 7
ROWS = 112
VMEM_BYTES = 54 * 2**20


def nn(a, b):
    return lax.dot_general(a, b, (((1,), (0,)), ((), ())), preferred_element_type=F32)


def nt(a, b):
    return lax.dot_general(a, b, (((1,), (1,)), ((), ())), preferred_element_type=F32)


def tn(a, b):
    return lax.dot_general(a, b, (((0,), (0,)), ((), ())), preferred_element_type=F32)


def normalize(v):
    centred = v - jnp.mean(v, axis=-1, keepdims=True)
    inverse = lax.rsqrt(jnp.mean(centred * centred, axis=-1, keepdims=True) + EPSILON)
    return centred * inverse, inverse


def norm_back(unit, inverse, gain, incoming):
    w = incoming * gain
    return inverse * (
        w - jnp.mean(w, axis=-1, keepdims=True) - unit * jnp.mean(w * unit, axis=-1, keepdims=True)
    )


def softmax(s):
    p = jnp.exp(s - jnp.max(s, axis=-1, keepdims=True))
    return p * (1.0 / jnp.sum(p, axis=-1, keepdims=True))


def fold8(v):
    total = v[0:8]
    for k in range(8, v.shape[0], 8):
        total = total + v[k : k + 8]
    return total


class Dims:
    def __init__(self, n_dp, n_mp, suffix, memory, group_kind, self_query, mlp_up):
        assert n_mp == 4
        self.n_dp = n_dp
        self.T, self.D = suffix.shape
        self.M = memory.shape[0]
        self.G = group_kind.shape[0]
        self.C = self_query.shape[1]
        self.F = mlp_up.shape[1]
        self.H = n_mp * self.C
        self.S = self.T // self.G
        self.K = self.M // self.G
        self.GO, self.RO, self.MO = self.G // 2, self.T // 2, self.M // 2
        self.NB = self.H // 256
        self.BLK = pl.cdiv(self.T, 128)
        self.TP = self.BLK * 128
        self.bits = n_dp.bit_length() - 1
        assert 1 << self.bits == n_dp and n_dp >= 4
        halvings = 0
        while halvings < self.bits and (self.D >> (halvings + 1)) % 16 == 0:
            halvings += 1
        self.halvings = halvings
        self.low = self.bits - halvings
        self.nch = 1 << halvings
        self.copies = 44 + 10 * self.bits
        self.rp = self.D // self.nch


UNITS = ("d1", "d2", "u1", "u2", "s1", "s2", "c1", "c2", "c3")
FOLDED = ("c2", "c3")
IN_NAMES = (
    "suffix",
    "memory",
    "cotangent",
    "kind",
    "prefix",
    "slen",
    "gain_self",
    "shift_self",
    "gain_cross",
    "shift_cross",
    "gain_mlp",
    "shift_mlp",
    "self_query",
    "self_key",
    "self_value",
    "self_out",
    "cross_query",
    "cross_key",
    "cross_value",
    "cross_out",
    "mlp_up",
    "mlp_down",
)
COUNTS, GAINS = IN_NAMES[3:6], IN_NAMES[6:12]
OUT_NAMES = (
    "layer_out",
    "suffix_grad",
    "memory_grad",
    "g_sq",
    "g_sk",
    "g_sv",
    "g_so",
    "g_cq",
    "g_ck",
    "g_cv",
    "g_co",
    "g_up",
    "g_dn",
    "norms",
)


def scratch(d):
    s = {}
    T, D, C, F, H, RO, MO, K = d.T, d.D, d.C, d.F, d.H, d.RO, d.MO, d.K

    def vmem(name, shape, dtype=BF):
        s[name] = pltpu.VMEM(shape, dtype)

    vmem("xin", (T, D))
    vmem("cot", (T, D))
    vmem("mem", (MO, D))
    vmem("wqkv", (3 * C, D))
    vmem("so", (C, D))
    for n in ("cq", "ck", "cv", "co"):
        vmem(n, (H, D))
    vmem("up", (D, F))
    vmem("dn", (F, D))
    vmem("a1", (T, D))
    for n in ("q1", "k1", "v1", "o1", "do1"):
        vmem(n, (d.TP, C))
    vmem("p1", (d.BLK, 3 * 128, 128))
    vmem("dqkv", (d.TP, 3 * C))
    for k in (1, 3, 4, 6):
        for n in ("s", "r", "xs", "xr"):
            vmem(f"{n}{k}", (RO, D))
    vmem("h1", (RO, D), F32)
    vmem("h2", (RO, D), F32)
    vmem("dh", (RO, D), F32)
    vmem("tmp", (RO, D), F32)
    vmem("a2", (RO, D))
    vmem("c2", (RO, D))
    for n in ("q2", "o2", "do2", "dq2"):
        vmem(n, (RO, H))
    for n in ("k2", "v2"):
        vmem(n, (MO, H))
    for n in ("p2", "ds2"):
        vmem(n, (d.GO * d.NB, 4 * d.S, K))
    vmem("a3", (T, D))
    vmem("c1", (T, D))
    vmem("act", (T, F))
    vmem("du", (T, F))
    vmem("dact", (T, F), F32)
    for u in UNITS:
        rows = d.rp // 2 if u in FOLDED else d.rp
        vmem("g_" + u + "_acc", (d.nch, rows, UNIT))
        if u[0] == "c":
            vmem("g_" + u + "_away", (d.nch, rows, UNIT))
            vmem("g_" + u + "_back", (d.nch, rows, UNIT))
        for k in range(d.halvings):
            vmem(f"g_{u}_r{k}", (d.nch >> (k + 1), rows, UNIT))
        for k in range(d.low):
            vmem(f"g_{u}_x{k}", (rows, UNIT))
            vmem(f"g_{u}_y{k}", (rows, UNIT))
    vmem("nst", (2 + d.bits, 8, D), F32)
    vmem("nrc", (1 + d.bits, 8, D), F32)
    for n in GAINS:
        s["v_" + n] = pltpu.VMEM((D,), F32)
    for n in COUNTS:
        s["n_" + n] = pltpu.SMEM((d.G,), jnp.int32)
    s["ss"] = pltpu.SemaphoreType.DMA((d.copies,))
    s["rs"] = pltpu.SemaphoreType.DMA((d.copies,))
    s["ls"] = pltpu.SemaphoreType.DMA((22,))
    return s


class Refs:
    pass


def kernel(d, names, *args):
    r = Refs()
    for name, ref in zip(names, args):
        setattr(r, name, ref)
    dp, mp = lax.axis_index("dp"), lax.axis_index("mp")
    core = lax.rem(mp, 2)
    sib = {"mp": mp + 1 - 2 * core}
    xmate = {"mp": lax.rem(mp + 2, 4)}
    own = pl.multiple_of(core * d.RO, 16)
    other = pl.multiple_of((1 - core) * d.RO, 16)
    own_rows, other_rows = pl.ds(own, d.RO), pl.ds(other, d.RO)
    factor = 1.0 / math.sqrt(HEAD)

    def bit_of(b):
        return lax.rem(dp // (1 << b), 2)

    def mate(b):
        return {"dp": dp + (1 << b) * (1 - 2 * bit_of(b))}

    corner = {"dp": dp + 3 - 2 * bit_of(0) - 4 * bit_of(1)}

    state = {"r": 0, "l": 0}
    sends = []

    def remote(src, dst, device, index=None):
        if index is None:
            index = state["r"]
            state["r"] += 1
        cp = pltpu.make_async_remote_copy(
            src_ref=src,
            dst_ref=dst,
            send_sem=r.ss.at[index],
            recv_sem=r.rs.at[index],
            device_id=device,
            device_id_type=MESH,
        )
        return cp

    def send(src, dst, device):
        cp = remote(src, dst, device)
        cp.start()
        sends.append(cp)
        return cp

    def load(src, dst):
        cp = pltpu.make_async_copy(src, dst, r.ls.at[state["l"]])
        state["l"] += 1
        cp.start()
        return cp

    barrier = pltpu.get_barrier_semaphore()
    mates = [sib, xmate, corner] + [mate(b) for b in range(d.bits)]
    for device in mates:
        pl.semaphore_signal(barrier, inc=1, device_id=device, device_id_type=MESH)
    ld = {}
    mp_rows = pl.ds(pl.multiple_of(mp * d.C, 16), d.C)
    ld["xin"] = load(r.suffix, r.xin)
    for n in GAINS[:2]:
        ld[n] = load(getattr(r, n), getattr(r, "v_" + n))
    ld["sq"] = load(r.self_query, r.wqkv.at[pl.ds(0, d.C)])
    ld["sk"] = load(r.self_key, r.wqkv.at[pl.ds(d.C, d.C)])
    ld["sv"] = load(r.self_value, r.wqkv.at[pl.ds(2 * d.C, d.C)])
    ld["ck"] = load(r.cross_key, r.ck.at[mp_rows])
    ld["cv"] = load(r.cross_value, r.cv.at[mp_rows])
    ld["cq"] = load(r.cross_query, r.cq.at[mp_rows])
    ld["co"] = load(r.cross_out, r.co.at[mp_rows])
    for n in COUNTS:
        ld[n] = load(getattr(r, n), getattr(r, "n_" + n))
    for n in GAINS[2:]:
        ld[n] = load(getattr(r, n), getattr(r, "v_" + n))
    ld["so"] = load(r.self_out, r.so)
    ld["cot"] = load(r.cotangent, r.cot)
    ld["dn"] = load(r.mlp_down, r.dn)
    ld["mem"] = load(r.memory.at[pl.ds(pl.multiple_of(core * d.MO, 16), d.MO)], r.mem)
    ld["up"] = load(r.mlp_up, r.up)

    PC = d.C // 4
    piece = lax.rem(dp, 4)
    full = {"ck": r.ck, "cv": r.cv, "cq": r.cq, "co": r.co}
    xm = lax.rem(mp + 2, 4)
    xm_rows = pl.ds(pl.multiple_of(xm * d.C, 16), d.C)
    gat = {}

    def part(ref, owner, which):
        return ref.at[pl.ds(pl.multiple_of(owner * d.C + which * PC, 16), PC)]

    def gather_start(w):
        ref = full[w]
        ld[w].wait()
        mine = part(ref, mp, piece)
        gat[w, "x"] = send(mine, mine, xmate)
        gat[w, "s"] = send(ref.at[mp_rows], ref.at[mp_rows], sib)

    def gather_x(w):
        gat[w, "x"].wait_recv()
        got = part(full[w], xm, piece)
        for k, device in enumerate((mate(0), mate(1), corner)):
            gat[w, k] = send(got, got, device)

    def gather_y(w):
        for k in range(3):
            gat[w, k].wait_recv()
        gat[w, "f"] = send(full[w].at[xm_rows], full[w].at[xm_rows], sib)

    def gather_done(w):
        gat[w, "s"].wait_recv()
        gat[w, "f"].wait_recv()


    class Unit:
        def __init__(self, name, finish, flip=0):
            self.name, self.finish, self.stage = name, finish, 0
            self.flip = flip
            self.acc = getattr(r, f"g_{name}_acc")
            self.base = 0
            self.cp = None

        def store(self, value, lane, acc=None):
            flip = self.flip
            if acc is None:
                acc = self.acc
            elif not isinstance(flip, int):
                flip = 1 - flip
            width = value.shape[1]
            half = d.rp // 2
            for j in range(d.nch):
                bits = [(j >> k) & 1 for k in range(d.halvings)]
                size = [d.nch >> (k + 1) for k in range(d.halvings)]
                p = sum(x * y for x, y in zip(bits, size))
                p = p + flip * (bits[1] - bits[0]) * (size[0] - size[1])
                part = value[j * d.rp : (j + 1) * d.rp].astype(BF)
                if self.name in FOLDED:
                    acc[p, :, :width] = part[:half]
                    acc[p, :, width:] = part[half:]
                else:
                    acc[p, :, lane : lane + width] = part

        def bit(self, k):
            if k > 1:
                return bit_of(d.low + k)
            near, far = bit_of(d.low + k), bit_of(d.low + 1 - k)
            return near + self.flip * (far - near)

        def mate(self, k):
            b = d.low + k
            step = (1 << b) * (1 - 2 * bit_of(b))
            if k < 2:
                c = d.low + 1 - k
                step = step + self.flip * ((1 << c) * (1 - 2 * bit_of(c)) - step)
            return {"dp": dp + step}

        def go(self):
            k = self.stage
            if k < d.halvings:
                half = d.nch >> (k + 1)
                dst = getattr(r, f"g_{self.name}_r{k}")
                src = self.acc.at[pl.ds(self.base + (1 - self.bit(k)) * half, half)]
                self.cp = send(src, dst, self.mate(k))
            else:
                e = k - d.halvings
                x = getattr(r, f"g_{self.name}_x{e}")
                x[...] = self.value.astype(BF)
                self.cp = send(x, getattr(r, f"g_{self.name}_y{e}"), mate(e))

        def step(self):
            k = self.stage
            self.cp.wait_recv()
            if k < d.halvings:
                half = d.nch >> (k + 1)
                got = getattr(r, f"g_{self.name}_r{k}")
                base = self.base + self.bit(k) * half
                self.base = base
                if k < d.halvings - 1:
                    for j in range(half):
                        self.acc[base + j] = (
                            self.acc[base + j].astype(F32) + got[j].astype(F32)
                        ).astype(BF)
                else:
                    self.value = self.acc[base].astype(F32) + got[0].astype(F32)
            else:
                e = k - d.halvings
                x = getattr(r, f"g_{self.name}_x{e}")
                y = getattr(r, f"g_{self.name}_y{e}")
                self.value = x[...].astype(F32) + y[...].astype(F32)
            self.stage += 1
            if self.stage < d.bits:
                self.go()
            else:
                self.finish(self.value)

        def drain(self):
            while self.stage < d.bits:
                self.step()

    def fin_dn(lane):
        def f(v):
            r.g_dn[:, lane : lane + UNIT] = v

        return f

    def fin_up(lane):
        def f(v):
            r.g_up[:, lane : lane + UNIT] = v

        return f

    def fin_pair(left, right, turn):
        def f(v):
            left[...] = v[:, : d.C]
            right[...] = v[:, d.C :].T if turn else v[:, d.C :]

        return f

    def fin_fold(ref):
        def f(v):
            ref[: d.rp // 2, :] = v[:, : d.C]
            ref[d.rp // 2 :, :] = v[:, d.C :]

        return f

    turn = core
    units = {
        "d1": Unit("d1", fin_dn(0), turn),
        "d2": Unit("d2", fin_dn(UNIT), 1 - turn),
        "u1": Unit("u1", fin_up(0), turn),
        "u2": Unit("u2", fin_up(UNIT), 1 - turn),
        "s1": Unit("s1", fin_pair(r.g_sq, r.g_sk, False), turn),
        "s2": Unit("s2", fin_pair(r.g_sv, r.g_so, True), 1 - turn),
        "c1": Unit("c1", fin_pair(r.g_cq, r.g_co, True), turn),
        "c2": Unit("c2", fin_fold(r.g_ck), turn),
        "c3": Unit("c3", fin_fold(r.g_cv), 1 - turn),
    }

    def steps(*which):
        for u in which:
            if units[u].stage < d.bits:
                units[u].step()

    def reduce_begin(k, partial):
        getattr(r, f"s{k}")[...] = partial(other_rows).astype(BF)
        return send(getattr(r, f"s{k}"), getattr(r, f"r{k}"), sib)

    def reduce_end(k, partial, cp):
        got, xs, xr = (getattr(r, f"{n}{k}") for n in ("r", "xs", "xr"))
        value = partial(own_rows)
        cp.wait_recv()
        xs[...] = (value + got[...].astype(F32)).astype(BF)
        return send(xs, xr, xmate)

    def total(k, s):
        return getattr(r, f"xs{k}")[s, :].astype(F32) + getattr(r, f"xr{k}")[s, :].astype(F32)

    def row_loop(n, body, carry=0):
        for i in range(0, n, ROWS):
            carry = body(i, carry)
        return carry

    def vec(name):
        return getattr(r, "v_" + name)[...].reshape(1, d.D)

    def head_masks(width, count):
        col = lax.broadcasted_iota(jnp.int32, (1, width), 1)
        f = [((col >= HEAD * h) & (col < HEAD * h + HEAD)).astype(F32) for h in range(count)]
        return f, [m.astype(BF) for m in f]

    HC = d.C // HEAD
    hf1, hb1 = head_masks(d.C, HC)
    hf2, hb2 = head_masks(256, 4)

    def spread(v, masks):
        return jnp.concatenate([v * m for m in masks], axis=0)

    def gatherh(v, masks):
        n = v.shape[0] // len(masks)
        out = v[:n] * masks[0]
        for h in range(1, len(masks)):
            out = out + v[h * n : (h + 1) * n] * masks[h]
        return out

    for n in ("q1", "k1", "v1", "o1", "do1"):
        ref = getattr(r, n)
        ref[d.T :, :] = jnp.zeros((d.TP - d.T, d.C), BF)
    for n in ("xin", *GAINS):
        ld[n].wait()
    gain, shift = vec("gain_self"), vec("shift_self")

    def norm_one(i, c):
        s = pl.ds(i, ROWS)
        z, _ = normalize(r.xin[s, :].astype(F32))
        r.a1[s, :] = (z * gain + shift).astype(BF)
        return c

    row_loop(d.T, norm_one)
    for n in ("sq", "sk", "sv"):
        ld[n].wait()
    qkv = nt(r.a1[...], r.wqkv[...])
    r.q1[: d.T, :] = (qkv[:, : d.C] * factor).astype(BF)
    r.k1[: d.T, :] = qkv[:, d.C : 2 * d.C].astype(BF)
    r.v1[: d.T, :] = qkv[:, 2 * d.C :].astype(BF)
    for n in COUNTS:
        ld[n].wait()
    pl.semaphore_wait(barrier, len(mates))
    for w in full:
        gather_start(w)

    ri = lax.broadcasted_iota(jnp.int32, (128, 128), 0)
    ci = lax.broadcasted_iota(jnp.int32, (128, 128), 1)
    near = (jnp.right_shift(ri, 5) == jnp.right_shift(ci, 5)) & (ci <= ri)
    place = jnp.bitwise_and(ci, 31)
    per = 128 // d.S
    tiles = [pl.ds(t * 128, 128) for t in range(d.BLK)]
    okays = []
    for t in range(d.BLK):
        lens = jnp.zeros((128, 128), jnp.int32)
        for k in range(per):
            g = t * per + k
            if g < d.G:
                lens = jnp.where(jnp.right_shift(ci, 5) == k, r.n_slen[g], lens)
        okays.append(near & (place < lens))
    sc = [nt(spread(r.q1[b, :], hb1), r.k1[b, :]) for b in tiles]
    sc = [
        jnp.concatenate(
            [jnp.where(ok, x[h * 128 : (h + 1) * 128], NEG_FILL) for h in range(HC)], axis=0
        )
        for x, ok in zip(sc, okays)
    ]
    top = [jnp.max(x, axis=-1, keepdims=True) for x in sc]
    sc = [jnp.exp(x - t) for x, t in zip(sc, top)]
    inv = [1.0 / jnp.sum(x, axis=-1, keepdims=True) for x in sc]
    sc = [(x * t).astype(BF) for x, t in zip(sc, inv)]
    out = [nn(x, r.v1[b, :]) for x, b in zip(sc, tiles)]
    for t, b in enumerate(tiles):
        r.p1[t] = sc[t]
        r.o1[b, :] = gatherh(out[t], hf1).astype(BF)
    gather_x("ck")
    ld["so"].wait()

    def out_one(rows):
        return nn(r.o1[rows, :], r.so[...])

    x1 = reduce_begin(1, out_one)
    ld["cot"].wait()
    ld["dn"].wait()
    r.dact[...] = nt(r.cot[...], r.dn[...])
    gather_x("cv")
    x1 = reduce_end(1, out_one, x1)

    gather_x("cq")
    ld["mem"].wait()
    big = d.MO // 2
    near_pair = pl.multiple_of((mp // 2) * 2 * d.C, 128)
    far_pair = pl.multiple_of(2 * d.C - (mp // 2) * 2 * d.C, 128)

    def project(w, dst, start):
        cols = pl.ds(start, 2 * d.C)

        for i in range(2):
            s = pl.ds(i * big, big)
            dst[s, cols] = nt(r.mem[s, :], w[cols, :]).astype(BF)

    gat["ck", "s"].wait_recv()
    project(r.ck, r.k2, near_pair)
    gather_x("co")
    gat["cv", "s"].wait_recv()
    project(r.cv, r.v2, near_pair)
    gather_y("ck")
    gat["ck", "f"].wait_recv()
    project(r.ck, r.k2, far_pair)
    gather_y("cv")
    gat["cv", "f"].wait_recv()
    project(r.cv, r.v2, far_pair)
    gather_y("cq")
    x1.wait_recv()
    gain, shift = vec("gain_cross"), vec("shift_cross")

    def norm_two(i, c):
        s = pl.ds(i, ROWS)
        h1 = r.xin[pl.ds(pl.multiple_of(own + i, 16), ROWS), :].astype(F32) + total(1, s)
        r.h1[s, :] = h1
        z, _ = normalize(h1)
        r.a2[s, :] = (z * gain + shift).astype(BF)
        return c

    row_loop(d.RO, norm_two)
    gather_done("cq")
    r.q2[...] = (nt(r.a2[...], r.cq[...]) * factor).astype(BF)
    slot = lax.broadcasted_iota(jnp.int32, (4 * d.S, d.K), 1)

    blocks = [slice(256 * b, 256 * b + 256) for b in range(d.NB)]

    def over_groups(body):
        for start in range(0, d.GO, GP):
            body(range(start, min(start + GP, d.GO)))

    def group_rows(g):
        return pl.ds(g * d.S, d.S), pl.ds(g * d.K, d.K)

    def cross_forward(groups):
        todo = [(g, k, *group_rows(g), b) for g in groups for k, b in enumerate(blocks)]
        n = [core * d.GO + g for g in groups]
        live = [r.n_kind[i] * PATCHES + r.n_prefix[i] for i in n]
        live = [x for x in live for b in blocks]
        v = [r.v2[ks, b] for g, k, qs, ks, b in todo]
        s = [nt(spread(r.q2[qs, b], hb2), r.k2[ks, b]) for g, k, qs, ks, b in todo]
        s = [jnp.where(slot < m, x, NEG_FILL) for x, m in zip(s, live)]
        top = [jnp.max(x, axis=-1, keepdims=True) for x in s]
        p = [jnp.exp(x - t) for x, t in zip(s, top)]
        scale = [1.0 / jnp.sum(x, axis=-1, keepdims=True) for x in p]
        p = [(x * t).astype(BF) for x, t in zip(p, scale)]
        o = [nn(x, y) for x, y in zip(p, v)]
        o = [gatherh(x, hf2).astype(BF) for x in o]
        for (g, k, qs, ks, b), x, y in zip(todo, p, o):
            r.p2[g * d.NB + k] = x
            r.o2[qs, b] = y

    over_groups(cross_forward)
    gather_y("co")
    gather_done("co")
    r.tmp[...] = nn(r.o2[...], r.co[...])
    gain, shift = vec("gain_mlp"), vec("shift_mlp")

    def norm_three(i, c):
        s = pl.ds(i, ROWS)
        h2 = r.h1[s, :] + r.tmp[s, :]
        r.h2[s, :] = h2
        z, _ = normalize(h2)
        r.a3[pl.ds(pl.multiple_of(own + i, 16), ROWS), :] = (z * gain + shift).astype(BF)
        return c

    row_loop(d.RO, norm_three)
    a3 = send(r.a3.at[own_rows], r.a3.at[own_rows], sib)

    ld["up"].wait()
    root = 1.0 / math.sqrt(2.0)
    bell = 1.0 / math.sqrt(2.0 * math.pi)

    def hidden(start):
        r.tmp[...] = nn(r.a3[pl.ds(start, d.RO), :], r.up[...])

        def body(i, c):
            u = r.tmp[pl.ds(i, ROWS), :]
            s = pl.ds(pl.multiple_of(start + i, 16), ROWS)
            half = 0.5 * (1.0 + lax.erf(u * root))
            r.act[s, :] = (u * half).astype(BF)
            slope = half + u * (bell * jnp.exp(-0.5 * u * u))
            r.du[s, :] = (r.dact[s, :] * slope).astype(BF)
            return c

        row_loop(d.RO, body)

    hidden(own)
    a3.wait_recv()
    hidden(other)

    def back_four(rows):
        return nt(r.du[rows, :], r.up[...])

    def out_three(rows):
        return nn(r.act[rows, :], r.dn[...])

    x4 = reduce_begin(4, back_four)
    for u, lane in (("d1", 0), ("d2", UNIT)):
        units[u].store(tn(r.cot[...], r.act[:, lane : lane + UNIT]), 0)
        units[u].go()
    x4 = reduce_end(4, back_four, x4)
    x3 = reduce_begin(3, out_three)
    for u, lane in (("u1", 0), ("u2", UNIT)):
        units[u].store(tn(r.a3[...], r.du[:, lane : lane + UNIT]), 0)
        units[u].go()
    x3 = reduce_end(3, out_three, x3)

    steps("d1", "d2")
    x4.wait_recv()
    gain = vec("gain_mlp")
    zero8 = jnp.zeros((8, d.D), F32)

    def back_three(i, c):
        gg, gs = c
        s = pl.ds(i, ROWS)
        e = total(4, s)
        z, inv = normalize(r.h2[s, :])
        dh = r.cot[pl.ds(pl.multiple_of(own + i, 16), ROWS), :].astype(F32) + norm_back(
            z, inv, gain, e
        )
        r.dh[s, :] = dh
        r.c2[s, :] = dh.astype(BF)
        return gg + fold8(e * z), gs + fold8(e)

    gain_mlp_grad, shift_mlp_grad = row_loop(d.RO, back_three, (zero8, zero8))
    r.do2[...] = nt(r.c2[...], r.co[...]).astype(BF)

    def cross_backward(groups):
        todo = [(g, k, *group_rows(g), b) for g in groups for k, b in enumerate(blocks)]
        k2 = [r.k2[ks, b] for g, k, qs, ks, b in todo]
        p = [r.p2[g * d.NB + k].astype(F32) for g, k, qs, ks, b in todo]
        t = [nt(spread(r.do2[qs, b], hb2), r.v2[ks, b]) for g, k, qs, ks, b in todo]
        t = [x * y for x, y in zip(p, t)]
        centre = [jnp.sum(x, axis=-1, keepdims=True) for x in t]
        ds = [(x - y * m).astype(BF) for x, y, m in zip(t, p, centre)]
        dq = [nn(x, y) for x, y in zip(ds, k2)]
        dq = [(gatherh(x, hf2) * factor).astype(BF) for x in dq]
        for (g, k, qs, ks, b), x, y in zip(todo, ds, dq):
            r.ds2[g * d.NB + k] = x
            r.dq2[qs, b] = y

    over_groups(cross_backward)
    r.tmp[...] = nn(r.dq2[...], r.cq[...])
    steps("u1", "u2")
    gain = vec("gain_cross")

    def back_two(i, c):
        gg, gs = c
        s = pl.ds(i, ROWS)
        e = r.tmp[s, :]
        z, inv = normalize(r.h1[s, :])
        dh = r.dh[s, :] + norm_back(z, inv, gain, e)
        r.dh[s, :] = dh
        r.c1[pl.ds(pl.multiple_of(own + i, 16), ROWS), :] = dh.astype(BF)
        return gg + fold8(e * z), gs + fold8(e)

    gain_cross_grad, shift_cross_grad = row_loop(d.RO, back_two, (zero8, zero8))
    c1 = send(r.c1.at[own_rows], r.c1.at[own_rows], sib)
    pair = pl.ds(pl.multiple_of((mp // 2) * 2 * d.C, 128), 2 * d.C)

    def split_columns(u, lane, value):
        left, right = value[:, : d.C], value[:, d.C :]
        first = core == 0
        units[u].store(jnp.where(first, left, right), lane)
        units[u].store(jnp.where(first, right, left), lane, getattr(r, f"g_{u}_away"))

    def swap(u):
        return send(getattr(r, f"g_{u}_away"), getattr(r, f"g_{u}_back"), sib)

    def merge(u, cp):
        unit, got = units[u], getattr(r, f"g_{u}_back")
        cp.wait_recv()
        for j in range(d.nch):
            unit.acc[j] = (unit.acc[j].astype(F32) + got[j].astype(F32)).astype(BF)
        unit.go()

    split_columns("c1", 0, tn(r.a2[...], r.dq2[:, pair]))
    split_columns("c1", d.C, tn(r.c2[...], r.o2[:, pair]))
    cc1 = swap("c1")
    r.do1[own_rows, :] = nt(r.c1[own_rows, :], r.so[...]).astype(BF)
    merge("c1", cc1)
    c1.wait_recv()
    r.do1[other_rows, :] = nt(r.c1[other_rows, :], r.so[...]).astype(BF)
    steps("d2", "d1")
    dom = [spread(r.do1[b, :], hb1) for b in tiles]
    tt = [nt(x, r.v1[b, :]) for x, b in zip(dom, tiles)]
    pb = [r.p1[t] for t in range(d.BLK)]
    pf = [x.astype(F32) for x in pb]
    tt = [x * y for x, y in zip(tt, pf)]
    mid = [jnp.sum(x, axis=-1, keepdims=True) for x in tt]
    ds = [(x - y * m).astype(BF) for x, y, m in zip(tt, pf, mid)]
    dq = [nn(x, r.k1[b, :]) for x, b in zip(ds, tiles)]
    dk = [tn(x, spread(r.q1[b, :], hb1)) for x, b in zip(ds, tiles)]
    dv = [tn(x, y) for x, y in zip(pb, dom)]
    for t, b in enumerate(tiles):
        r.dqkv[b, : d.C] = (gatherh(dq[t], hf1) * factor).astype(BF)
        r.dqkv[b, d.C : 2 * d.C] = dk[t].astype(BF)
        r.dqkv[b, 2 * d.C :] = dv[t].astype(BF)

    def back_six(rows):
        return nn(r.dqkv[rows, :], r.wqkv[...])

    rows = slice(0, d.T)
    x6 = reduce_begin(6, back_six)
    units["s1"].store(tn(r.a1[...], r.dqkv[rows, : 2 * d.C]), 0)
    units["s1"].go()
    x6 = reduce_end(6, back_six, x6)
    units["s2"].store(tn(r.a1[...], r.dqkv[rows, 2 * d.C :]), 0)
    units["s2"].store(tn(r.c1[...], r.o1[rows, :]), d.C)
    units["s2"].go()

    def cross_keys(left, right, dst):
        def body(groups):
            todo = [(g, k, *group_rows(g), b) for g in groups for k, b in enumerate(blocks)]
            out = [
                tn(left[g * d.NB + k], spread(right[qs, b], hb2)).astype(BF)
                for g, k, qs, ks, b in todo
            ]
            for (g, k, qs, ks, b), x in zip(todo, out):
                dst[ks, b] = x

        over_groups(body)

    cross_keys(r.ds2, r.q2, r.k2)
    split_columns("c2", 0, tn(r.mem[...], r.k2[:, pair]))
    cc2 = swap("c2")
    steps("u2", "u1")
    cross_keys(r.p2, r.do2, r.v2)
    merge("c2", cc2)
    split_columns("c3", 0, tn(r.mem[...], r.v2[:, pair]))
    cc3 = swap("c3")
    x3.wait_recv()

    def finish_out(i, c):
        s = pl.ds(i, ROWS)
        r.layer_out[pl.ds(pl.multiple_of(own + i, 16), ROWS), :] = (r.h2[s, :] + total(3, s)).astype(BF)
        return c

    row_loop(d.RO, finish_out)
    tail = [send(r.layer_out.at[own_rows], r.layer_out.at[own_rows], sib)]
    merge("c3", cc3)
    steps("d2", "c1", "d1")

    x6.wait_recv()
    gain = vec("gain_self")

    def back_one(i, c):
        gg, gs = c
        s = pl.ds(i, ROWS)
        e = total(6, s)
        z, inv = normalize(r.xin[pl.ds(pl.multiple_of(own + i, 16), ROWS), :].astype(F32))
        r.suffix_grad[pl.ds(pl.multiple_of(own + i, 16), ROWS), :] = (
            r.dh[s, :] + norm_back(z, inv, gain, e)
        ).astype(BF)
        return gg + fold8(e * z), gs + fold8(e)

    gain_self_grad, shift_self_grad = row_loop(d.RO, back_one, (zero8, zero8))
    tail.append(send(r.suffix_grad.at[own_rows], r.suffix_grad.at[own_rows], sib))
    for k, v in enumerate(
        (
            gain_self_grad,
            shift_self_grad,
            gain_cross_grad,
            shift_cross_grad,
            gain_mlp_grad,
            shift_mlp_grad,
        )
    ):
        r.nst[0, k : k + 1, :] = jnp.sum(v, axis=0, keepdims=True)
    r.nst[0, 6:8, :] = jnp.zeros((2, d.D), F32)
    devices = [sib] + [mate(b) for b in range(d.bits)]
    ncp = send(r.nst.at[0], r.nrc.at[0], devices[0])

    def norm_step(k, cp):
        cp.wait_recv()
        r.nst[k + 1] = r.nst[k] + r.nrc[k]
        if k + 1 < len(devices):
            return send(r.nst.at[k + 1], r.nrc.at[k + 1], devices[k + 1])
        return None

    parts = 4
    base_r = state["r"]
    state["r"] += parts
    piece_rows = d.MO // parts

    def memory_copy(i):
        rows = pl.ds(pl.multiple_of(core * d.MO + i * piece_rows, 16), piece_rows)
        return remote(r.memory_grad.at[rows], r.memory_grad.at[rows], sib, base_r + i)

    def memory_part(i):
        s = pl.ds(i * piece_rows, piece_rows)
        there = pl.ds(pl.multiple_of(core * d.MO + i * piece_rows, 16), piece_rows)
        value = nn(r.k2[s, :], r.ck[...]) + nn(r.v2[s, :], r.cv[...])
        r.memory_grad[there, :] = value.astype(BF)
        memory_copy(i).start()

    memory_part(0)
    memory_part(1)
    steps("s1", "u2")
    ncp = norm_step(0, ncp)
    memory_part(2)
    memory_part(3)
    ncp = norm_step(1, ncp)
    k = 2
    for u in ("u1", "c1", "s2", "s1", "c2", "c1", "c3", "s1", "s2", "c2", "c3", "s2", "c2", "c3"):
        steps(u)
        if u == "c2" and ncp is not None:
            ncp = norm_step(k, ncp)
            k += 1
    while ncp is not None:
        ncp = norm_step(k, ncp)
        k += 1
    r.norms[...] = r.nst[len(devices)]
    while any(unit.stage < d.bits for unit in units.values()):
        steps(*units)
    for i in range(parts):
        memory_copy(i).wait()
    for cp in tail:
        cp.wait_recv()
    for cp in sends:
        cp.wait_send()
    assert state["r"] == d.copies


def solution(mesh):
    n_dp, n_mp = mesh.shape["dp"], mesh.shape["mp"]

    def on_device(*args):
        d = Dims(n_dp, n_mp, args[0], args[1], args[3], args[12], args[20])
        assert d.C * 2 == UNIT and d.F == 2 * UNIT
        scr = scratch(d)
        names = IN_NAMES + OUT_NAMES + tuple(scr)
        col, turned = (d.rp, d.C), (d.C, d.rp)
        shapes = [
            ((d.T, d.D), BF),
            ((d.T, d.D), BF),
            ((d.M, d.D), BF),
            (col, F32),
            (col, F32),
            (col, F32),
            (turned, F32),
            (col, F32),
            (col, F32),
            (col, F32),
            (turned, F32),
            ((d.rp, d.F), F32),
            ((d.rp, d.F), F32),
            ((8, d.D), F32),
        ]
        hbm, vmem = pl.BlockSpec(memory_space=pl.ANY), pl.BlockSpec(memory_space=pltpu.VMEM)

        def body(*refs):
            kernel(d, names, *refs)

        outs = pl.pallas_call(
            body,
            out_shape=[pltpu.VMEM(*s) for s in shapes],
            in_specs=[hbm] * 22,
            out_specs=[vmem] * 14,
            scratch_shapes=list(scr.values()),
            compiler_params=pltpu.CompilerParams(
                collective_id=0, has_side_effects=True, vmem_limit_bytes=VMEM_BYTES
            ),
            name="layer",
        )(*(a.T if k in (12, 13, 14, 16, 17, 18) else a for k, a in enumerate(args)))
        outs = [pltpu.with_memory_space_constraint(o, pltpu.VMEM) for o in outs]
        rows = d.D // n_dp

        def write(*refs):
            ins, norms, dst, vectors, sem = refs[:13], refs[13], refs[14:27], refs[27:33], refs[33]
            cut = d.M // 8
            pieces = [(ins[2].at[pl.ds(k * cut, cut)], dst[2].at[pl.ds(k * cut, cut)]) for k in range(8)]
            pieces += [(a, b) for k, (a, b) in enumerate(zip(ins, dst)) if k != 2]
            copies = [pltpu.make_async_copy(a, b, sem.at[k]) for k, (a, b) in enumerate(pieces)]
            for cp in copies:
                cp.start()
            shift = lax.rem(d.D - lax.axis_index("dp") * rows, d.D)
            mine = pltpu.roll(norms[...], shift, 1)
            for k, v in enumerate(vectors):
                v[...] = mine[k, :rows]
            for cp in copies:
                cp.wait()

        final = pl.pallas_call(
            write,
            out_shape=[jax.ShapeDtypeStruct(*s) for s in shapes[:13]]
            + [jax.ShapeDtypeStruct((rows,), F32)] * 6,
            in_specs=[vmem] * 14,
            out_specs=[hbm] * 13 + [vmem] * 6,
            scratch_shapes=[pltpu.SemaphoreType.DMA((20,))],
            compiler_params=pltpu.CompilerParams(vmem_limit_bytes=2**20),
            name="write",
        )(*outs)
        big, grads, vectors = final[:3], list(final[3:13]), final[13:]
        dp = lax.axis_index("dp")
        if d.low:
            start = lax.rem(dp, 1 << d.low) * rows
            for k, turn in enumerate((0, 0, 0, 1, 0, 0, 0, 1, 0, 0)):
                grads[k] = lax.dynamic_slice_in_dim(grads[k], start, rows, axis=turn)
        grads[9] = grads[9].T
        return (*big, *grads, *vectors)

    row, col, turn = P("dp", None), P("dp", "mp"), P("mp", "dp")
    wide, tall = P(None, "mp"), P("mp", None)
    in_specs = (row,) * 3 + (P("dp"),) * 3 + (P(),) * 6
    in_specs += (wide, wide, wide, tall, wide, wide, wide, tall, wide, tall)
    out_specs = (row,) * 3 + (col, col, col, turn, col, col, col, turn, col, turn)
    out_specs += (P("dp"),) * 6
    return jax.shard_map(
        on_device, mesh=mesh, in_specs=in_specs, out_specs=out_specs, check_vma=False
    )
```

```python
import math

import jax
import jax.numpy as jnp
from jax import lax
from jax.experimental import pallas as pl
from jax.experimental.pallas import tpu as pltpu
from jax.sharding import PartitionSpec as P

BF = jnp.bfloat16
F32 = jnp.float32
MESH = pl.DeviceIdType.MESH
HEAD = 64
PATCHES = 196
EPSILON = 1e-06
NEG_FILL = -1e30
UNIT = 384
GP = 7
ROWS = 112
VMEM_BYTES = 54 * 2**20


def nn(a, b):
    return lax.dot_general(a, b, (((1,), (0,)), ((), ())), preferred_element_type=F32)


def nt(a, b):
    return lax.dot_general(a, b, (((1,), (1,)), ((), ())), preferred_element_type=F32)


def tn(a, b):
    return lax.dot_general(a, b, (((0,), (0,)), ((), ())), preferred_element_type=F32)


def normalize(v):
    centred = v - jnp.mean(v, axis=-1, keepdims=True)
    inverse = lax.rsqrt(jnp.mean(centred * centred, axis=-1, keepdims=True) + EPSILON)
    return centred * inverse, inverse


def norm_back(unit, inverse, gain, incoming):
    w = incoming * gain
    return inverse * (
        w - jnp.mean(w, axis=-1, keepdims=True) - unit * jnp.mean(w * unit, axis=-1, keepdims=True)
    )


def softmax(s):
    p = jnp.exp(s - jnp.max(s, axis=-1, keepdims=True))
    return p * (1.0 / jnp.sum(p, axis=-1, keepdims=True))


def fold8(v):
    total = v[0:8]
    for k in range(8, v.shape[0], 8):
        total = total + v[k : k + 8]
    return total


class Dims:
    def __init__(self, n_dp, n_mp, suffix, memory, group_kind, self_query, mlp_up):
        assert n_mp == 4
        self.n_dp = n_dp
        self.T, self.D = suffix.shape
        self.M = memory.shape[0]
        self.G = group_kind.shape[0]
        self.C = self_query.shape[1]
        self.F = mlp_up.shape[1]
        self.H = n_mp * self.C
        self.S = self.T // self.G
        self.K = self.M // self.G
        self.GO, self.RO, self.MO = self.G // 2, self.T // 2, self.M // 2
        self.NB = self.H // 256
        self.BLK = pl.cdiv(self.T, 128)
        self.TP = self.BLK * 128
        self.bits = n_dp.bit_length() - 1
        assert 1 << self.bits == n_dp and n_dp >= 4
        halvings = 0
        while halvings < self.bits and (self.D >> (halvings + 1)) % 16 == 0:
            halvings += 1
        self.halvings = halvings
        self.low = self.bits - halvings
        self.nch = 1 << halvings
        self.copies = 44 + 10 * self.bits
        self.rp = self.D // self.nch


UNITS = ("d1", "d2", "u1", "u2", "s1", "s2", "c1", "c2", "c3")
FOLDED = ("c2", "c3")
IN_NAMES = (
    "suffix",
    "memory",
    "cotangent",
    "kind",
    "prefix",
    "slen",
    "gain_self",
    "shift_self",
    "gain_cross",
    "shift_cross",
    "gain_mlp",
    "shift_mlp",
    "self_query",
    "self_key",
    "self_value",
    "self_out",
    "cross_query",
    "cross_key",
    "cross_value",
    "cross_out",
    "mlp_up",
    "mlp_down",
)
COUNTS, GAINS = IN_NAMES[3:6], IN_NAMES[6:12]
OUT_NAMES = (
    "layer_out",
    "suffix_grad",
    "memory_grad",
    "g_sq",
    "g_sk",
    "g_sv",
    "g_so",
    "g_cq",
    "g_ck",
    "g_cv",
    "g_co",
    "g_up",
    "g_dn",
    "norms",
)


def scratch(d):
    s = {}
    T, D, C, F, H, RO, MO, K = d.T, d.D, d.C, d.F, d.H, d.RO, d.MO, d.K

    def vmem(name, shape, dtype=BF):
        s[name] = pltpu.VMEM(shape, dtype)

    vmem("xin", (T, D))
    vmem("cot", (T, D))
    vmem("mem", (MO, D))
    vmem("wqkv", (3 * C, D))
    vmem("so", (C, D))
    for n in ("cq", "ck", "cv", "co"):
        vmem(n, (H, D))
    vmem("up", (D, F))
    vmem("dn", (F, D))
    vmem("a1", (T, D))
    for n in ("q1", "k1", "v1", "o1", "do1"):
        vmem(n, (d.TP, C))
    vmem("p1", (d.BLK, 3 * 128, 128))
    vmem("dqkv", (d.TP, 3 * C))
    for k in (1, 3, 4, 6):
        for n in ("s", "r", "xs", "xr"):
            vmem(f"{n}{k}", (RO, D))
    vmem("h1", (RO, D), F32)
    vmem("h2", (RO, D), F32)
    vmem("dh", (RO, D), F32)
    vmem("tmp", (RO, D), F32)
    vmem("a2", (RO, D))
    vmem("c2", (RO, D))
    for n in ("q2", "o2", "do2", "dq2"):
        vmem(n, (RO, H))
    for n in ("k2", "v2"):
        vmem(n, (MO, H))
    for n in ("p2", "ds2"):
        vmem(n, (d.GO * d.NB, 4 * d.S, K))
    vmem("a3", (T, D))
    vmem("c1", (T, D))
    vmem("act", (T, F))
    vmem("du", (T, F))
    vmem("dact", (T, F), F32)
    for u in UNITS:
        rows = d.rp // 2 if u in FOLDED else d.rp
        vmem("g_" + u + "_acc", (d.nch, rows, UNIT))
        if u[0] == "c":
            vmem("g_" + u + "_away", (d.nch, rows, UNIT))
            vmem("g_" + u + "_back", (d.nch, rows, UNIT))
        for k in range(d.halvings):
            vmem(f"g_{u}_r{k}", (d.nch >> (k + 1), rows, UNIT))
        for k in range(d.low):
            vmem(f"g_{u}_x{k}", (rows, UNIT))
            vmem(f"g_{u}_y{k}", (rows, UNIT))
    vmem("nst", (2 + d.bits, 8, D), F32)
    vmem("nrc", (1 + d.bits, 8, D), F32)
    for n in GAINS:
        s["v_" + n] = pltpu.VMEM((D,), F32)
    for n in COUNTS:
        s["n_" + n] = pltpu.SMEM((d.G,), jnp.int32)
    s["ss"] = pltpu.SemaphoreType.DMA((d.copies,))
    s["rs"] = pltpu.SemaphoreType.DMA((d.copies,))
    s["ls"] = pltpu.SemaphoreType.DMA((22,))
    return s


class Refs:
    pass


def kernel(d, names, *args):
    r = Refs()
    for name, ref in zip(names, args):
        setattr(r, name, ref)
    dp, mp = lax.axis_index("dp"), lax.axis_index("mp")
    core = lax.rem(mp, 2)
    sib = {"mp": mp + 1 - 2 * core}
    xmate = {"mp": lax.rem(mp + 2, 4)}
    own = pl.multiple_of(core * d.RO, 16)
    other = pl.multiple_of((1 - core) * d.RO, 16)
    own_rows, other_rows = pl.ds(own, d.RO), pl.ds(other, d.RO)
    factor = 1.0 / math.sqrt(HEAD)

    def bit_of(b):
        return lax.rem(dp // (1 << b), 2)

    def mate(b):
        return {"dp": dp + (1 << b) * (1 - 2 * bit_of(b))}

    corner = {"dp": dp + 3 - 2 * bit_of(0) - 4 * bit_of(1)}

    state = {"r": 0, "l": 0}
    sends = []

    def remote(src, dst, device, index=None):
        if index is None:
            index = state["r"]
            state["r"] += 1
        cp = pltpu.make_async_remote_copy(
            src_ref=src,
            dst_ref=dst,
            send_sem=r.ss.at[index],
            recv_sem=r.rs.at[index],
            device_id=device,
            device_id_type=MESH,
        )
        return cp

    def send(src, dst, device):
        cp = remote(src, dst, device)
        cp.start()
        sends.append(cp)
        return cp

    def load(src, dst):
        cp = pltpu.make_async_copy(src, dst, r.ls.at[state["l"]])
        state["l"] += 1
        cp.start()
        return cp

    barrier = pltpu.get_barrier_semaphore()
    mates = [sib, xmate, corner] + [mate(b) for b in range(d.bits)]
    for device in mates:
        pl.semaphore_signal(barrier, inc=1, device_id=device, device_id_type=MESH)
    ld = {}
    mp_rows = pl.ds(pl.multiple_of(mp * d.C, 16), d.C)
    ld["xin"] = load(r.suffix, r.xin)
    for n in GAINS[:2]:
        ld[n] = load(getattr(r, n), getattr(r, "v_" + n))
    ld["sq"] = load(r.self_query, r.wqkv.at[pl.ds(0, d.C)])
    ld["sk"] = load(r.self_key, r.wqkv.at[pl.ds(d.C, d.C)])
    ld["sv"] = load(r.self_value, r.wqkv.at[pl.ds(2 * d.C, d.C)])
    ld["ck"] = load(r.cross_key, r.ck.at[mp_rows])
    ld["cv"] = load(r.cross_value, r.cv.at[mp_rows])
    ld["cq"] = load(r.cross_query, r.cq.at[mp_rows])
    ld["co"] = load(r.cross_out, r.co.at[mp_rows])
    for n in COUNTS:
        ld[n] = load(getattr(r, n), getattr(r, "n_" + n))
    for n in GAINS[2:]:
        ld[n] = load(getattr(r, n), getattr(r, "v_" + n))
    ld["so"] = load(r.self_out, r.so)
    ld["cot"] = load(r.cotangent, r.cot)
    ld["dn"] = load(r.mlp_down, r.dn)
    ld["mem"] = load(r.memory.at[pl.ds(pl.multiple_of(core * d.MO, 16), d.MO)], r.mem)
    ld["up"] = load(r.mlp_up, r.up)

    PC = d.C // 4
    piece = lax.rem(dp, 4)
    full = {"ck": r.ck, "cv": r.cv, "cq": r.cq, "co": r.co}
    xm = lax.rem(mp + 2, 4)
    xm_rows = pl.ds(pl.multiple_of(xm * d.C, 16), d.C)
    gat = {}

    def part(ref, owner, which):
        return ref.at[pl.ds(pl.multiple_of(owner * d.C + which * PC, 16), PC)]

    def gather_start(w):
        ref = full[w]
        ld[w].wait()
        mine = part(ref, mp, piece)
        gat[w, "x"] = send(mine, mine, xmate)
        gat[w, "s"] = send(ref.at[mp_rows], ref.at[mp_rows], sib)

    def gather_x(w):
        gat[w, "x"].wait_recv()
        got = part(full[w], xm, piece)
        for k, device in enumerate((mate(0), mate(1), corner)):
            gat[w, k] = send(got, got, device)

    def gather_y(w):
        for k in range(3):
            gat[w, k].wait_recv()
        gat[w, "f"] = send(full[w].at[xm_rows], full[w].at[xm_rows], sib)

    def gather_done(w):
        gat[w, "s"].wait_recv()
        gat[w, "f"].wait_recv()


    class Unit:
        def __init__(self, name, finish, flip=0):
            self.name, self.finish, self.stage = name, finish, 0
            self.flip = flip
            self.acc = getattr(r, f"g_{name}_acc")
            self.base = 0
            self.cp = None

        def store(self, value, lane, acc=None):
            flip = self.flip
            if acc is None:
                acc = self.acc
            elif not isinstance(flip, int):
                flip = 1 - flip
            width = value.shape[1]
            half = d.rp // 2
            for j in range(d.nch):
                bits = [(j >> k) & 1 for k in range(d.halvings)]
                size = [d.nch >> (k + 1) for k in range(d.halvings)]
                p = sum(x * y for x, y in zip(bits, size))
                p = p + flip * (bits[1] - bits[0]) * (size[0] - size[1])
                part = value[j * d.rp : (j + 1) * d.rp].astype(BF)
                if self.name in FOLDED:
                    acc[p, :, :width] = part[:half]
                    acc[p, :, width:] = part[half:]
                else:
                    acc[p, :, lane : lane + width] = part

        def bit(self, k):
            if k > 1:
                return bit_of(d.low + k)
            near, far = bit_of(d.low + k), bit_of(d.low + 1 - k)
            return near + self.flip * (far - near)

        def mate(self, k):
            b = d.low + k
            step = (1 << b) * (1 - 2 * bit_of(b))
            if k < 2:
                c = d.low + 1 - k
                step = step + self.flip * ((1 << c) * (1 - 2 * bit_of(c)) - step)
            return {"dp": dp + step}

        def go(self):
            k = self.stage
            if k < d.halvings:
                half = d.nch >> (k + 1)
                dst = getattr(r, f"g_{self.name}_r{k}")
                src = self.acc.at[pl.ds(self.base + (1 - self.bit(k)) * half, half)]
                self.cp = send(src, dst, self.mate(k))
            else:
                e = k - d.halvings
                x = getattr(r, f"g_{self.name}_x{e}")
                x[...] = self.value.astype(BF)
                self.cp = send(x, getattr(r, f"g_{self.name}_y{e}"), mate(e))

        def step(self):
            k = self.stage
            self.cp.wait_recv()
            if k < d.halvings:
                half = d.nch >> (k + 1)
                got = getattr(r, f"g_{self.name}_r{k}")
                base = self.base + self.bit(k) * half
                self.base = base
                if k < d.halvings - 1:
                    for j in range(half):
                        self.acc[base + j] = (
                            self.acc[base + j].astype(F32) + got[j].astype(F32)
                        ).astype(BF)
                else:
                    self.value = self.acc[base].astype(F32) + got[0].astype(F32)
            else:
                e = k - d.halvings
                x = getattr(r, f"g_{self.name}_x{e}")
                y = getattr(r, f"g_{self.name}_y{e}")
                self.value = x[...].astype(F32) + y[...].astype(F32)
            self.stage += 1
            if self.stage < d.bits:
                self.go()
            else:
                self.finish(self.value)

        def drain(self):
            while self.stage < d.bits:
                self.step()

    def fin_dn(lane):
        def f(v):
            r.g_dn[:, lane : lane + UNIT] = v

        return f

    def fin_up(lane):
        def f(v):
            r.g_up[:, lane : lane + UNIT] = v

        return f

    def fin_pair(left, right, turn):
        def f(v):
            left[...] = v[:, : d.C]
            right[...] = v[:, d.C :].T if turn else v[:, d.C :]

        return f

    def fin_fold(ref):
        def f(v):
            ref[: d.rp // 2, :] = v[:, : d.C]
            ref[d.rp // 2 :, :] = v[:, d.C :]

        return f

    turn = core
    units = {
        "d1": Unit("d1", fin_dn(0), turn),
        "d2": Unit("d2", fin_dn(UNIT), 1 - turn),
        "u1": Unit("u1", fin_up(0), turn),
        "u2": Unit("u2", fin_up(UNIT), 1 - turn),
        "s1": Unit("s1", fin_pair(r.g_sq, r.g_sk, False), turn),
        "s2": Unit("s2", fin_pair(r.g_sv, r.g_so, True), 1 - turn),
        "c1": Unit("c1", fin_pair(r.g_cq, r.g_co, True), turn),
        "c2": Unit("c2", fin_fold(r.g_ck), 0),
        "c3": Unit("c3", fin_fold(r.g_cv), 0),
    }

    def steps(*which):
        for u in which:
            if units[u].stage < d.bits:
                units[u].step()

    def reduce_begin(k, partial):
        getattr(r, f"s{k}")[...] = partial(other_rows).astype(BF)
        return send(getattr(r, f"s{k}"), getattr(r, f"r{k}"), sib)

    def reduce_end(k, partial, cp):
        got, xs, xr = (getattr(r, f"{n}{k}") for n in ("r", "xs", "xr"))
        value = partial(own_rows)
        cp.wait_recv()
        xs[...] = (value + got[...].astype(F32)).astype(BF)
        return send(xs, xr, xmate)

    def total(k, s):
        return getattr(r, f"xs{k}")[s, :].astype(F32) + getattr(r, f"xr{k}")[s, :].astype(F32)

    def row_loop(n, body, carry=0):
        for i in range(0, n, ROWS):
            carry = body(i, carry)
        return carry

    def vec(name):
        return getattr(r, "v_" + name)[...].reshape(1, d.D)

    def head_masks(width, count):
        col = lax.broadcasted_iota(jnp.int32, (1, width), 1)
        f = [((col >= HEAD * h) & (col < HEAD * h + HEAD)).astype(F32) for h in range(count)]
        return f, [m.astype(BF) for m in f]

    HC = d.C // HEAD
    hf1, hb1 = head_masks(d.C, HC)
    hf2, hb2 = head_masks(256, 4)

    def spread(v, masks):
        return jnp.concatenate([v * m for m in masks], axis=0)

    def gatherh(v, masks):
        n = v.shape[0] // len(masks)
        out = v[:n] * masks[0]
        for h in range(1, len(masks)):
            out = out + v[h * n : (h + 1) * n] * masks[h]
        return out

    for n in ("q1", "k1", "v1", "o1", "do1"):
        ref = getattr(r, n)
        ref[d.T :, :] = jnp.zeros((d.TP - d.T, d.C), BF)
    for n in ("xin", *GAINS):
        ld[n].wait()
    gain, shift = vec("gain_self"), vec("shift_self")

    def norm_one(i, c):
        s = pl.ds(i, ROWS)
        z, _ = normalize(r.xin[s, :].astype(F32))
        r.a1[s, :] = (z * gain + shift).astype(BF)
        return c

    row_loop(d.T, norm_one)
    for n in ("sq", "sk", "sv"):
        ld[n].wait()
    qkv = nt(r.a1[...], r.wqkv[...])
    r.q1[: d.T, :] = (qkv[:, : d.C] * factor).astype(BF)
    r.k1[: d.T, :] = qkv[:, d.C : 2 * d.C].astype(BF)
    r.v1[: d.T, :] = qkv[:, 2 * d.C :].astype(BF)
    for n in COUNTS:
        ld[n].wait()
    pl.semaphore_wait(barrier, len(mates))
    for w in full:
        gather_start(w)

    ri = lax.broadcasted_iota(jnp.int32, (128, 128), 0)
    ci = lax.broadcasted_iota(jnp.int32, (128, 128), 1)
    near = (jnp.right_shift(ri, 5) == jnp.right_shift(ci, 5)) & (ci <= ri)
    place = jnp.bitwise_and(ci, 31)
    per = 128 // d.S
    tiles = [pl.ds(t * 128, 128) for t in range(d.BLK)]
    okays = []
    for t in range(d.BLK):
        lens = jnp.zeros((128, 128), jnp.int32)
        for k in range(per):
            g = t * per + k
            if g < d.G:
                lens = jnp.where(jnp.right_shift(ci, 5) == k, r.n_slen[g], lens)
        okays.append(near & (place < lens))
    sc = [nt(spread(r.q1[b, :], hb1), r.k1[b, :]) for b in tiles]
    sc = [
        jnp.concatenate(
            [jnp.where(ok, x[h * 128 : (h + 1) * 128], NEG_FILL) for h in range(HC)], axis=0
        )
        for x, ok in zip(sc, okays)
    ]
    top = [jnp.max(x, axis=-1, keepdims=True) for x in sc]
    sc = [jnp.exp(x - t) for x, t in zip(sc, top)]
    inv = [1.0 / jnp.sum(x, axis=-1, keepdims=True) for x in sc]
    sc = [(x * t).astype(BF) for x, t in zip(sc, inv)]
    out = [nn(x, r.v1[b, :]) for x, b in zip(sc, tiles)]
    for t, b in enumerate(tiles):
        r.p1[t] = sc[t]
        r.o1[b, :] = gatherh(out[t], hf1).astype(BF)
    gather_x("ck")
    ld["so"].wait()

    def out_one(rows):
        return nn(r.o1[rows, :], r.so[...])

    x1 = reduce_begin(1, out_one)
    ld["cot"].wait()
    ld["dn"].wait()
    r.dact[...] = nt(r.cot[...], r.dn[...])
    gather_x("cv")
    x1 = reduce_end(1, out_one, x1)

    gather_x("cq")
    ld["mem"].wait()
    big = d.MO // 2
    near_pair = pl.multiple_of((mp // 2) * 2 * d.C, 128)
    far_pair = pl.multiple_of(2 * d.C - (mp // 2) * 2 * d.C, 128)

    def project(w, dst, start):
        cols = pl.ds(start, 2 * d.C)

        for i in range(2):
            s = pl.ds(i * big, big)
            dst[s, cols] = nt(r.mem[s, :], w[cols, :]).astype(BF)

    gat["ck", "s"].wait_recv()
    project(r.ck, r.k2, near_pair)
    gather_x("co")
    gat["cv", "s"].wait_recv()
    project(r.cv, r.v2, near_pair)
    gather_y("ck")
    gat["ck", "f"].wait_recv()
    project(r.ck, r.k2, far_pair)
    gather_y("cv")
    gat["cv", "f"].wait_recv()
    project(r.cv, r.v2, far_pair)
    gather_y("cq")
    x1.wait_recv()
    gain, shift = vec("gain_cross"), vec("shift_cross")

    def norm_two(i, c):
        s = pl.ds(i, ROWS)
        h1 = r.xin[pl.ds(pl.multiple_of(own + i, 16), ROWS), :].astype(F32) + total(1, s)
        r.h1[s, :] = h1
        z, _ = normalize(h1)
        r.a2[s, :] = (z * gain + shift).astype(BF)
        return c

    row_loop(d.RO, norm_two)
    gather_done("cq")
    r.q2[...] = (nt(r.a2[...], r.cq[...]) * factor).astype(BF)
    slot = lax.broadcasted_iota(jnp.int32, (4 * d.S, d.K), 1)

    blocks = [slice(256 * b, 256 * b + 256) for b in range(d.NB)]

    def over_groups(body):
        for start in range(0, d.GO, GP):
            body(range(start, min(start + GP, d.GO)))

    def group_rows(g):
        return pl.ds(g * d.S, d.S), pl.ds(g * d.K, d.K)

    def cross_forward(groups):
        todo = [(g, k, *group_rows(g), b) for g in groups for k, b in enumerate(blocks)]
        n = [core * d.GO + g for g in groups]
        live = [r.n_kind[i] * PATCHES + r.n_prefix[i] for i in n]
        live = [x for x in live for b in blocks]
        v = [r.v2[ks, b] for g, k, qs, ks, b in todo]
        s = [nt(spread(r.q2[qs, b], hb2), r.k2[ks, b]) for g, k, qs, ks, b in todo]
        s = [jnp.where(slot < m, x, NEG_FILL) for x, m in zip(s, live)]
        top = [jnp.max(x, axis=-1, keepdims=True) for x in s]
        p = [jnp.exp(x - t) for x, t in zip(s, top)]
        scale = [1.0 / jnp.sum(x, axis=-1, keepdims=True) for x in p]
        p = [(x * t).astype(BF) for x, t in zip(p, scale)]
        o = [nn(x, y) for x, y in zip(p, v)]
        o = [gatherh(x, hf2).astype(BF) for x in o]
        for (g, k, qs, ks, b), x, y in zip(todo, p, o):
            r.p2[g * d.NB + k] = x
            r.o2[qs, b] = y

    over_groups(cross_forward)
    gather_y("co")
    gather_done("co")
    r.tmp[...] = nn(r.o2[...], r.co[...])
    gain, shift = vec("gain_mlp"), vec("shift_mlp")

    def norm_three(i, c):
        s = pl.ds(i, ROWS)
        h2 = r.h1[s, :] + r.tmp[s, :]
        r.h2[s, :] = h2
        z, _ = normalize(h2)
        r.a3[pl.ds(pl.multiple_of(own + i, 16), ROWS), :] = (z * gain + shift).astype(BF)
        return c

    row_loop(d.RO, norm_three)
    a3 = send(r.a3.at[own_rows], r.a3.at[own_rows], sib)

    ld["up"].wait()
    root = 1.0 / math.sqrt(2.0)
    bell = 1.0 / math.sqrt(2.0 * math.pi)

    def hidden(start):
        r.tmp[...] = nn(r.a3[pl.ds(start, d.RO), :], r.up[...])

        def body(i, c):
            u = r.tmp[pl.ds(i, ROWS), :]
            s = pl.ds(pl.multiple_of(start + i, 16), ROWS)
            half = 0.5 * (1.0 + lax.erf(u * root))
            r.act[s, :] = (u * half).astype(BF)
            slope = half + u * (bell * jnp.exp(-0.5 * u * u))
            r.du[s, :] = (r.dact[s, :] * slope).astype(BF)
            return c

        row_loop(d.RO, body)

    hidden(own)
    a3.wait_recv()
    hidden(other)

    def back_four(rows):
        return nt(r.du[rows, :], r.up[...])

    def out_three(rows):
        return nn(r.act[rows, :], r.dn[...])

    x4 = reduce_begin(4, back_four)
    for u, lane in (("d1", 0), ("d2", UNIT)):
        units[u].store(tn(r.cot[...], r.act[:, lane : lane + UNIT]), 0)
        units[u].go()
    x4 = reduce_end(4, back_four, x4)
    x3 = reduce_begin(3, out_three)
    for u, lane in (("u1", 0), ("u2", UNIT)):
        units[u].store(tn(r.a3[...], r.du[:, lane : lane + UNIT]), 0)
        units[u].go()
    x3 = reduce_end(3, out_three, x3)

    steps("d1", "d2")
    x4.wait_recv()
    gain = vec("gain_mlp")
    zero8 = jnp.zeros((8, d.D), F32)

    def back_three(i, c):
        gg, gs = c
        s = pl.ds(i, ROWS)
        e = total(4, s)
        z, inv = normalize(r.h2[s, :])
        dh = r.cot[pl.ds(pl.multiple_of(own + i, 16), ROWS), :].astype(F32) + norm_back(
            z, inv, gain, e
        )
        r.dh[s, :] = dh
        r.c2[s, :] = dh.astype(BF)
        return gg + fold8(e * z), gs + fold8(e)

    gain_mlp_grad, shift_mlp_grad = row_loop(d.RO, back_three, (zero8, zero8))
    r.do2[...] = nt(r.c2[...], r.co[...]).astype(BF)

    def cross_backward(groups):
        todo = [(g, k, *group_rows(g), b) for g in groups for k, b in enumerate(blocks)]
        k2 = [r.k2[ks, b] for g, k, qs, ks, b in todo]
        p = [r.p2[g * d.NB + k].astype(F32) for g, k, qs, ks, b in todo]
        t = [nt(spread(r.do2[qs, b], hb2), r.v2[ks, b]) for g, k, qs, ks, b in todo]
        t = [x * y for x, y in zip(p, t)]
        centre = [jnp.sum(x, axis=-1, keepdims=True) for x in t]
        ds = [(x - y * m).astype(BF) for x, y, m in zip(t, p, centre)]
        dq = [nn(x, y) for x, y in zip(ds, k2)]
        dq = [(gatherh(x, hf2) * factor).astype(BF) for x in dq]
        for (g, k, qs, ks, b), x, y in zip(todo, ds, dq):
            r.ds2[g * d.NB + k] = x
            r.dq2[qs, b] = y

    over_groups(cross_backward)
    r.tmp[...] = nn(r.dq2[...], r.cq[...])
    steps("u1", "u2")
    gain = vec("gain_cross")

    def back_two(i, c):
        gg, gs = c
        s = pl.ds(i, ROWS)
        e = r.tmp[s, :]
        z, inv = normalize(r.h1[s, :])
        dh = r.dh[s, :] + norm_back(z, inv, gain, e)
        r.dh[s, :] = dh
        r.c1[pl.ds(pl.multiple_of(own + i, 16), ROWS), :] = dh.astype(BF)
        return gg + fold8(e * z), gs + fold8(e)

    gain_cross_grad, shift_cross_grad = row_loop(d.RO, back_two, (zero8, zero8))
    c1 = send(r.c1.at[own_rows], r.c1.at[own_rows], sib)
    pair = pl.ds(pl.multiple_of((mp // 2) * 2 * d.C, 128), 2 * d.C)

    def split_columns(u, lane, value):
        left, right = value[:, : d.C], value[:, d.C :]
        first = core == 0
        units[u].store(jnp.where(first, left, right), lane)
        units[u].store(jnp.where(first, right, left), lane, getattr(r, f"g_{u}_away"))

    def swap(u):
        return send(getattr(r, f"g_{u}_away"), getattr(r, f"g_{u}_back"), sib)

    def merge(u, cp):
        unit, got = units[u], getattr(r, f"g_{u}_back")
        cp.wait_recv()
        for j in range(d.nch):
            unit.acc[j] = (unit.acc[j].astype(F32) + got[j].astype(F32)).astype(BF)
        unit.go()

    split_columns("c1", 0, tn(r.a2[...], r.dq2[:, pair]))
    split_columns("c1", d.C, tn(r.c2[...], r.o2[:, pair]))
    cc1 = swap("c1")
    r.do1[own_rows, :] = nt(r.c1[own_rows, :], r.so[...]).astype(BF)
    merge("c1", cc1)
    c1.wait_recv()
    r.do1[other_rows, :] = nt(r.c1[other_rows, :], r.so[...]).astype(BF)
    steps("d2", "d1")
    dom = [spread(r.do1[b, :], hb1) for b in tiles]
    tt = [nt(x, r.v1[b, :]) for x, b in zip(dom, tiles)]
    pb = [r.p1[t] for t in range(d.BLK)]
    pf = [x.astype(F32) for x in pb]
    tt = [x * y for x, y in zip(tt, pf)]
    mid = [jnp.sum(x, axis=-1, keepdims=True) for x in tt]
    ds = [(x - y * m).astype(BF) for x, y, m in zip(tt, pf, mid)]
    dq = [nn(x, r.k1[b, :]) for x, b in zip(ds, tiles)]
    dk = [tn(x, spread(r.q1[b, :], hb1)) for x, b in zip(ds, tiles)]
    dv = [tn(x, y) for x, y in zip(pb, dom)]
    for t, b in enumerate(tiles):
        r.dqkv[b, : d.C] = (gatherh(dq[t], hf1) * factor).astype(BF)
        r.dqkv[b, d.C : 2 * d.C] = dk[t].astype(BF)
        r.dqkv[b, 2 * d.C :] = dv[t].astype(BF)

    def back_six(rows):
        return nn(r.dqkv[rows, :], r.wqkv[...])

    rows = slice(0, d.T)
    x6 = reduce_begin(6, back_six)
    units["s1"].store(tn(r.a1[...], r.dqkv[rows, : 2 * d.C]), 0)
    units["s1"].go()
    x6 = reduce_end(6, back_six, x6)
    units["s2"].store(tn(r.a1[...], r.dqkv[rows, 2 * d.C :]), 0)
    units["s2"].store(tn(r.c1[...], r.o1[rows, :]), d.C)
    units["s2"].go()

    def cross_keys(left, right, dst):
        def body(groups):
            todo = [(g, k, *group_rows(g), b) for g in groups for k, b in enumerate(blocks)]
            out = [
                tn(left[g * d.NB + k], spread(right[qs, b], hb2)).astype(BF)
                for g, k, qs, ks, b in todo
            ]
            for (g, k, qs, ks, b), x in zip(todo, out):
                dst[ks, b] = x

        over_groups(body)

    cross_keys(r.ds2, r.q2, r.k2)
    split_columns("c2", 0, tn(r.mem[...], r.k2[:, pair]))
    cc2 = swap("c2")
    steps("u2", "u1")
    cross_keys(r.p2, r.do2, r.v2)
    merge("c2", cc2)
    split_columns("c3", 0, tn(r.mem[...], r.v2[:, pair]))
    cc3 = swap("c3")
    x3.wait_recv()

    def finish_out(i, c):
        s = pl.ds(i, ROWS)
        r.layer_out[pl.ds(pl.multiple_of(own + i, 16), ROWS), :] = (r.h2[s, :] + total(3, s)).astype(BF)
        return c

    row_loop(d.RO, finish_out)
    tail = [send(r.layer_out.at[own_rows], r.layer_out.at[own_rows], sib)]
    merge("c3", cc3)
    steps("d2", "c1", "d1")

    x6.wait_recv()
    gain = vec("gain_self")

    def back_one(i, c):
        gg, gs = c
        s = pl.ds(i, ROWS)
        e = total(6, s)
        z, inv = normalize(r.xin[pl.ds(pl.multiple_of(own + i, 16), ROWS), :].astype(F32))
        r.suffix_grad[pl.ds(pl.multiple_of(own + i, 16), ROWS), :] = (
            r.dh[s, :] + norm_back(z, inv, gain, e)
        ).astype(BF)
        return gg + fold8(e * z), gs + fold8(e)

    gain_self_grad, shift_self_grad = row_loop(d.RO, back_one, (zero8, zero8))
    tail.append(send(r.suffix_grad.at[own_rows], r.suffix_grad.at[own_rows], sib))
    for k, v in enumerate(
        (
            gain_self_grad,
            shift_self_grad,
            gain_cross_grad,
            shift_cross_grad,
            gain_mlp_grad,
            shift_mlp_grad,
        )
    ):
        r.nst[0, k : k + 1, :] = jnp.sum(v, axis=0, keepdims=True)
    r.nst[0, 6:8, :] = jnp.zeros((2, d.D), F32)
    devices = [sib] + [mate(b) for b in range(d.bits)]
    ncp = send(r.nst.at[0], r.nrc.at[0], devices[0])

    def norm_step(k, cp):
        cp.wait_recv()
        r.nst[k + 1] = r.nst[k] + r.nrc[k]
        if k + 1 < len(devices):
            return send(r.nst.at[k + 1], r.nrc.at[k + 1], devices[k + 1])
        return None

    parts = 4
    base_r = state["r"]
    state["r"] += parts
    piece_rows = d.MO // parts

    def memory_copy(i):
        rows = pl.ds(pl.multiple_of(core * d.MO + i * piece_rows, 16), piece_rows)
        return remote(r.memory_grad.at[rows], r.memory_grad.at[rows], sib, base_r + i)

    def memory_part(i):
        s = pl.ds(i * piece_rows, piece_rows)
        there = pl.ds(pl.multiple_of(core * d.MO + i * piece_rows, 16), piece_rows)
        value = nn(r.k2[s, :], r.ck[...]) + nn(r.v2[s, :], r.cv[...])
        r.memory_grad[there, :] = value.astype(BF)
        memory_copy(i).start()

    memory_part(0)
    memory_part(1)
    steps("s1", "u2")
    ncp = norm_step(0, ncp)
    memory_part(2)
    memory_part(3)
    ncp = norm_step(1, ncp)
    k = 2
    for u in ("u1", "c1", "s2", "s1", "c2", "c1", "c3", "s1", "s2", "c2", "c3", "s2", "c2", "c3"):
        steps(u)
        if u == "c2" and ncp is not None:
            ncp = norm_step(k, ncp)
            k += 1
    while ncp is not None:
        ncp = norm_step(k, ncp)
        k += 1
    r.norms[...] = r.nst[len(devices)]
    while any(unit.stage < d.bits for unit in units.values()):
        steps(*units)
    for i in range(parts):
        memory_copy(i).wait()
    for cp in tail:
        cp.wait_recv()
    for cp in sends:
        cp.wait_send()
    assert state["r"] == d.copies


def solution(mesh):
    n_dp, n_mp = mesh.shape["dp"], mesh.shape["mp"]

    def on_device(*args):
        d = Dims(n_dp, n_mp, args[0], args[1], args[3], args[12], args[20])
        assert d.C * 2 == UNIT and d.F == 2 * UNIT
        scr = scratch(d)
        names = IN_NAMES + OUT_NAMES + tuple(scr)
        col, turned = (d.rp, d.C), (d.C, d.rp)
        shapes = [
            ((d.T, d.D), BF),
            ((d.T, d.D), BF),
            ((d.M, d.D), BF),
            (col, F32),
            (col, F32),
            (col, F32),
            (turned, F32),
            (col, F32),
            (col, F32),
            (col, F32),
            (turned, F32),
            ((d.rp, d.F), F32),
            ((d.rp, d.F), F32),
            ((8, d.D), F32),
        ]
        hbm, vmem = pl.BlockSpec(memory_space=pl.ANY), pl.BlockSpec(memory_space=pltpu.VMEM)

        def body(*refs):
            kernel(d, names, *refs)

        outs = pl.pallas_call(
            body,
            out_shape=[pltpu.VMEM(*s) for s in shapes],
            in_specs=[hbm] * 22,
            out_specs=[vmem] * 14,
            scratch_shapes=list(scr.values()),
            compiler_params=pltpu.CompilerParams(
                collective_id=0, has_side_effects=True, vmem_limit_bytes=VMEM_BYTES
            ),
            name="layer",
        )(*(a.T if k in (12, 13, 14, 16, 17, 18) else a for k, a in enumerate(args)))
        outs = [pltpu.with_memory_space_constraint(o, pltpu.VMEM) for o in outs]
        rows = d.D // n_dp

        def write(*refs):
            ins, norms, dst, vectors, sem = refs[:13], refs[13], refs[14:27], refs[27:33], refs[33]
            cut = d.M // 8
            pieces = [(ins[2].at[pl.ds(k * cut, cut)], dst[2].at[pl.ds(k * cut, cut)]) for k in range(8)]
            pieces += [(a, b) for k, (a, b) in enumerate(zip(ins, dst)) if k != 2]
            copies = [pltpu.make_async_copy(a, b, sem.at[k]) for k, (a, b) in enumerate(pieces)]
            for cp in copies:
                cp.start()
            shift = lax.rem(d.D - lax.axis_index("dp") * rows, d.D)
            mine = pltpu.roll(norms[...], shift, 1)
            for k, v in enumerate(vectors):
                v[...] = mine[k, :rows]
            for cp in copies:
                cp.wait()

        final = pl.pallas_call(
            write,
            out_shape=[jax.ShapeDtypeStruct(*s) for s in shapes[:13]]
            + [jax.ShapeDtypeStruct((rows,), F32)] * 6,
            in_specs=[vmem] * 14,
            out_specs=[hbm] * 13 + [vmem] * 6,
            scratch_shapes=[pltpu.SemaphoreType.DMA((20,))],
            compiler_params=pltpu.CompilerParams(vmem_limit_bytes=2**20),
            name="write",
        )(*outs)
        big, grads, vectors = final[:3], list(final[3:13]), final[13:]
        dp = lax.axis_index("dp")
        if d.low:
            start = lax.rem(dp, 1 << d.low) * rows
            for k, turn in enumerate((0, 0, 0, 1, 0, 0, 0, 1, 0, 0)):
                grads[k] = lax.dynamic_slice_in_dim(grads[k], start, rows, axis=turn)
        grads[9] = grads[9].T
        return (*big, *grads, *vectors)

    row, col, turn = P("dp", None), P("dp", "mp"), P("mp", "dp")
    wide, tall = P(None, "mp"), P("mp", None)
    in_specs = (row,) * 3 + (P("dp"),) * 3 + (P(),) * 6
    in_specs += (wide, wide, wide, tall, wide, wide, wide, tall, wide, tall)
    out_specs = (row,) * 3 + (col, col, col, turn, col, col, col, turn, col, turn)
    out_specs += (P("dp"),) * 6
    return jax.shard_map(
        on_device, mesh=mesh, in_specs=in_specs, out_specs=out_specs, check_vma=False
    )
```
